32 devices in a mesh: parts: 1, rows: 8 (over z, y), branch: 2 (over core), head: 2 (over x).
Axes of the slice: x: 2, y: 2, z: 4, core: 2. Of those that a mesh axis runs over, the one named last changes fastest.
Arguments:
- lineup_state: bfloat16 [32, 128, 256], P(('parts', 'rows', 'branch')), may hold values from -12 to 12
- pairwise: bfloat16 [128, 128, 128], P(('parts', 'rows', 'branch')), may hold values from -12 to 12
- aligned_residue_bounds: int32 [32, 2], P('parts'), may hold values from 0 to 128, as said below
- residue_valid_mask: int32 [128], P('parts'), may hold values from 0 to 1, as said below
- coupling_offset_weight_map: bfloat16 [128, 8], P(None, 'head'), may hold values from -0.5 to 0.5
- triangle_bias_matrix: bfloat16 [128, 4], P(None, 'head'), may hold values from -0.5 to 0.5
- alignment_projection_matrix: bfloat16 [4, 256, 256], P(None, None, 'head'), may hold values from -1 to 1
- lineup_readout_weight: bfloat16 [256, 256], replicated, may hold values from -4 to 4
- feedfwd_entry_weight: bfloat16 [256, 1024], P(None, 'head'), may hold values from -0.375 to 0.375
- feedfwd_exit_weight: bfloat16 [1024, 256], P('head'), may hold values from -0.1875 to 0.1875
- pair_projection_matrix: bfloat16 [4, 128, 128], P(None, None, 'head'), may hold values from -2 to 2
- pair_output_matrix: bfloat16 [128, 128], P(None, 'head'), may hold values from -6 to 6
- left_right_maps: bfloat16 [2, 256, 32], replicated, may hold values from -0.375 to 0.375
- outer_product_output_matrix: bfloat16 [1024, 128], P(None, 'head'), may hold values from -1.5 to 1.5
Outputs:
- refreshed_lineup_state: bfloat16 [32, 128, 256], P(('parts', 'rows', 'branch'), None, 'head')
- pairwise_out: bfloat16 [128, 128, 128], P(('parts', 'rows', 'branch'), None, 'head')
The draws below stay inside these ranges and needn't reach their ends.
Inputs may be any that keep to these rules, and one draw needn't show every extreme that they name: `aligned_residue_bounds`: each row holds a start below its end; row 0 covers all 128 residues; every span covers a quarter of the 128 residues or more and starts in the first half. `residue_valid_mask`: 1 on a prefix that holds at least half of the 128 residues, 0 after it; the last residue is always 0.
All inputs are finite; a program needn't handle non-finite values.
Results may differ from the reference program's by a relative error of at most 0.011.
Values may be sent and summed in bfloat16 or wider, within the bound.
No kernel may reach another device: no remote copies, remote signals or barrier semaphores. Data moves between devices by JAX's collectives and lax.ppermute only.
A program may use at most 64 MiB of HBM per device.

```python
import math
import jax
import jax.numpy as jnp
from jax import lax

LINEUP_DEPTH = 256
COUPLING_DEPTH = 128
LINEUP_FOCI = 8
HZ = 4
PER_FOCUS_DIM = 32
OPM_DEPTH = 32
FEEDFWD_UNITS = 1024
LINEUP_STRANDS = 32
CHAIN_SPAN = 128


def raised_strands(key, lead, width):
    noise = jax.random.truncated_normal(jax.random.fold_in(key, 31), -6.0, 6.0, (lead, CHAIN_SPAN, width), jnp.float32)
    return noise


def raised_coefficient(key, width, features):
    base = jax.random.truncated_normal(jax.random.fold_in(key, 41), -4.0, 4.0, (4, width, features), jnp.float32) * width ** (-0.5)
    return base


def draw_lineup_state(key, part):
    return raised_strands(jax.random.fold_in(key, 5), LINEUP_STRANDS, LINEUP_DEPTH).astype(jnp.bfloat16)


def draw_pairwise(key, part):
    return raised_strands(jax.random.fold_in(key, 7), CHAIN_SPAN, COUPLING_DEPTH).astype(jnp.bfloat16)


def draw_alignment_projection_matrix(key, part):
    return raised_coefficient(jax.random.fold_in(key, 13), LINEUP_DEPTH, LINEUP_FOCI * PER_FOCUS_DIM).astype(jnp.bfloat16)


def draw_pair_projection_matrix(key, part):
    return raised_coefficient(jax.random.fold_in(key, 17), COUPLING_DEPTH, HZ * PER_FOCUS_DIM).astype(jnp.bfloat16)


def draw_aligned_residue_bounds(key, part):
    opening_draw_seed, closing_draw_seed = jax.random.split(jax.random.fold_in(key, 11))
    stretch_begin = jax.random.randint(opening_draw_seed, (LINEUP_STRANDS,), 0, CHAIN_SPAN // 2)
    stretch_extent = jax.random.randint(closing_draw_seed, (LINEUP_STRANDS,), CHAIN_SPAN // 4, CHAIN_SPAN + 1)
    span_end = jnp.minimum(stretch_begin + stretch_extent, CHAIN_SPAN)
    stretch_begin = stretch_begin.at[0].set(0)
    span_end = span_end.at[0].set(CHAIN_SPAN)
    return jnp.stack([stretch_begin, span_end], axis=1).astype(jnp.int32)


def draw_residue_valid_mask(key, part):
    valid_count = jax.random.randint(jax.random.fold_in(key, 23), (), CHAIN_SPAN // 2, CHAIN_SPAN)
    return (jnp.arange(CHAIN_SPAN, dtype=jnp.int32) < valid_count).astype(jnp.int32)


def level_of(own_key, shape, pieces, smallest, high):
    def one(axis_at, blocks):
        draws = jax.random.uniform(jax.random.fold_in(jax.random.fold_in(own_key, 6), axis_at), (blocks,), jnp.float32, smallest / len(pieces), high / len(pieces))
        return jnp.repeat(jnp.exp(draws), shape[axis_at] // blocks).reshape((-1,) + (1,) * (len(shape) - axis_at - 1))

    gain = one(*pieces[0])
    for cut in pieces[1:]:
        gain = gain * one(*cut)
    return gain


def bell_draw(own_key, dims, scale, reach, cuts=(), held_as=jnp.bfloat16):
    drawn = scale * jax.random.normal(own_key, dims, jnp.float32)
    if cuts:
        drawn = drawn * level_of(own_key, dims, cuts, -0.22, 0.18)
    return jnp.clip(drawn, -reach, reach).astype(held_as)


def setup_inputs(seed: int = 0, part: int = 0) -> dict:
    streams_of = jax.random.split(jax.random.key(seed), 15)
    part_keys = jax.random.split(jax.random.fold_in(streams_of[14], part), 15)
    return {
        "lineup_state": draw_lineup_state(jax.random.fold_in(jax.random.fold_in(streams_of[14], part), 71), part),
        "pairwise": draw_pairwise(jax.random.fold_in(jax.random.fold_in(streams_of[14], part), 71), part),
        "aligned_residue_bounds": draw_aligned_residue_bounds(jax.random.fold_in(jax.random.fold_in(streams_of[14], part), 71), part),
        "residue_valid_mask": draw_residue_valid_mask(jax.random.fold_in(jax.random.fold_in(streams_of[14], part), 71), part),
        "coupling_offset_weight_map": bell_draw(streams_of[4], (COUPLING_DEPTH, LINEUP_FOCI), COUPLING_DEPTH ** -0.5, 0.5, ((1, 2),)),
        "triangle_bias_matrix": bell_draw(streams_of[5], (COUPLING_DEPTH, HZ), COUPLING_DEPTH ** -0.5, 0.5, ((1, 2),)),
        "alignment_projection_matrix": draw_alignment_projection_matrix(jax.random.fold_in(streams_of[14], 71), part),
        "lineup_readout_weight": bell_draw(streams_of[7], (LINEUP_FOCI * PER_FOCUS_DIM, LINEUP_DEPTH), (max(1, LINEUP_FOCI * PER_FOCUS_DIM // 128)) ** -0.5, 4.0),
        "feedfwd_entry_weight": bell_draw(streams_of[8], (LINEUP_DEPTH, FEEDFWD_UNITS), LINEUP_DEPTH ** -0.5, 0.375, ((1, 2),)),
        "feedfwd_exit_weight": bell_draw(streams_of[9], (FEEDFWD_UNITS, LINEUP_DEPTH), FEEDFWD_UNITS ** -0.5, 0.1875, ((0, 2),)),
        "pair_projection_matrix": draw_pair_projection_matrix(jax.random.fold_in(streams_of[14], 71), part),
        "pair_output_matrix": bell_draw(streams_of[11], (HZ * PER_FOCUS_DIM, COUPLING_DEPTH), (max(1, HZ * PER_FOCUS_DIM // 128)) ** -0.5, 6.0, ((1, 2),)),
        "left_right_maps": bell_draw(streams_of[12], (2, LINEUP_DEPTH, OPM_DEPTH), LINEUP_DEPTH ** -0.5, 0.375),
        "outer_product_output_matrix": bell_draw(streams_of[13], (OPM_DEPTH * OPM_DEPTH, COUPLING_DEPTH), (OPM_DEPTH * OPM_DEPTH // 64) ** -0.5, 1.5, ((1, 2),)),
    }


def layer_normalize(values):
    values = values.astype(jnp.float32)
    center = values - lax.optimization_barrier(jnp.mean(values, -1, keepdims=True))
    spread = lax.optimization_barrier(jnp.mean(center * center, -1, keepdims=True))
    return center * lax.rsqrt(spread + 1e-05)

def soft_weights(attention_scores):
    row_max = lax.optimization_barrier(jnp.max(attention_scores, -1, keepdims=True))
    shifted = jnp.exp(attention_scores - row_max)
    return shifted / lax.optimization_barrier(jnp.sum(shifted, -1, keepdims=True))

def reference(lineup_state, pairwise, aligned_residue_bounds, residue_valid_mask, coupling_offset_weight_map, triangle_bias_matrix, alignment_projection_matrix, lineup_readout_weight, feedfwd_entry_weight, feedfwd_exit_weight, pair_projection_matrix, pair_output_matrix, left_right_maps, outer_product_output_matrix):
    places = jnp.arange(CHAIN_SPAN, dtype=jnp.int32)
    inside = (places[None, :] >= aligned_residue_bounds[:, 0:1]) & (places[None, :] < aligned_residue_bounds[:, 1:2])
    sequence_mask = inside.astype(jnp.float32)
    key_valid = residue_valid_mask > 0
    inv_scale = 1.0 / math.sqrt(PER_FOCUS_DIM)
    alignment_normed = layer_normalize(lineup_state).astype(jnp.bfloat16)
    pair_normed = layer_normalize(pairwise).astype(jnp.bfloat16)
    alignment_bias = jnp.einsum('tue,el->ltu', pair_normed.astype(jnp.float32), coupling_offset_weight_map.astype(jnp.float32)).astype(jnp.bfloat16)
    tri_bias = jnp.einsum('tue,el->ltu', pair_normed.astype(jnp.float32), triangle_bias_matrix.astype(jnp.float32)).astype(jnp.bfloat16)
    lineup_mapped = jnp.einsum('tvf,xfp->xtvp', alignment_normed.astype(jnp.float32), alignment_projection_matrix.astype(jnp.float32))
    lineup_probe_lookup_content = lineup_mapped[:3].astype(jnp.bfloat16).reshape(3, LINEUP_STRANDS, CHAIN_SPAN, LINEUP_FOCI, PER_FOCUS_DIM)
    alignment_gate = jax.nn.sigmoid(lineup_mapped[3])

    def alignment_row(row_elements):
        row_query, row_key, strand_content, gate_row, mask_row = row_elements
        attention_scores = jnp.einsum('ihd,jhd->hij', row_query.astype(jnp.float32), row_key.astype(jnp.float32)) * inv_scale
        attention_scores = attention_scores + alignment_bias.astype(jnp.float32)
        attention_scores = jnp.where(mask_row[None, None, :] > 0, attention_scores, -1000000000.0)
        softmax_shares = soft_weights(attention_scores).astype(jnp.bfloat16)
        mixed_strand = jnp.einsum('ftv,vfn->tfn', softmax_shares.astype(jnp.float32), strand_content.astype(jnp.float32)).reshape(CHAIN_SPAN, LINEUP_FOCI * PER_FOCUS_DIM)
        return (mixed_strand * gate_row).astype(jnp.bfloat16)
    lineup_focus_split = lax.map(alignment_row, (lineup_probe_lookup_content[0], lineup_probe_lookup_content[1], lineup_probe_lookup_content[2], alignment_gate, sequence_mask))
    lineup_blended = lineup_state.astype(jnp.float32) + jnp.dot(lineup_focus_split.reshape(LINEUP_STRANDS * CHAIN_SPAN, LINEUP_FOCI * PER_FOCUS_DIM), lineup_readout_weight, preferred_element_type=jnp.float32).reshape(LINEUP_STRANDS, CHAIN_SPAN, LINEUP_DEPTH)
    feedfwd_standardized = layer_normalize(lineup_blended).astype(jnp.bfloat16)
    feedfwd_inner = jax.nn.relu(jnp.dot(feedfwd_standardized.reshape(LINEUP_STRANDS * CHAIN_SPAN, LINEUP_DEPTH), feedfwd_entry_weight, preferred_element_type=jnp.float32)).astype(jnp.bfloat16)
    refreshed_lineup_state = (lineup_blended + jnp.dot(feedfwd_inner, feedfwd_exit_weight, preferred_element_type=jnp.float32).reshape(LINEUP_STRANDS, CHAIN_SPAN, LINEUP_DEPTH)).astype(jnp.bfloat16)

    def tri_row(z_row):
        row_proj = jnp.einsum('jc,gcd->gjd', z_row.astype(jnp.float32), pair_projection_matrix.astype(jnp.float32))
        row_qkv = row_proj[:3].astype(jnp.bfloat16).reshape(3, CHAIN_SPAN, HZ, PER_FOCUS_DIM)
        attention_scores = jnp.einsum('jhd,khd->hjk', row_qkv[0].astype(jnp.float32), row_qkv[1].astype(jnp.float32)) * inv_scale
        attention_scores = attention_scores + tri_bias.astype(jnp.float32)
        attention_scores = jnp.where(key_valid[None, None, :], attention_scores, -1000000000.0)
        softmax_shares = soft_weights(attention_scores).astype(jnp.bfloat16)
        mixed_strand = jnp.einsum('hjk,khd->jhd', softmax_shares.astype(jnp.float32), row_qkv[2].astype(jnp.float32)).reshape(CHAIN_SPAN, HZ * PER_FOCUS_DIM)
        return (mixed_strand * jax.nn.sigmoid(row_proj[3])).astype(jnp.bfloat16)
    pairwise_heads = lax.map(tri_row, pair_normed)
    tri_update = jnp.dot(pairwise_heads.reshape(CHAIN_SPAN * CHAIN_SPAN, HZ * PER_FOCUS_DIM), pair_output_matrix, preferred_element_type=jnp.float32).reshape(CHAIN_SPAN, CHAIN_SPAN, COUPLING_DEPTH)
    outer_factors = (jnp.einsum('juf,bfn->bjun', alignment_normed.astype(jnp.float32), left_right_maps.astype(jnp.float32)) * sequence_mask[None, :, :, None]).astype(jnp.bfloat16)
    pair_count = jnp.dot(sequence_mask.T, sequence_mask, precision=lax.Precision.HIGHEST)
    col_factors = outer_factors[1].astype(jnp.float32)

    def opm_row(row_elements):
        row_factor, counts = row_elements
        outer_sum = jnp.einsum('sp,sjq->jpq', row_factor.astype(jnp.float32), col_factors)
        outer_mean = (outer_sum / counts[:, None, None]).astype(jnp.bfloat16)
        return jnp.dot(outer_mean.reshape(CHAIN_SPAN, OPM_DEPTH * OPM_DEPTH), outer_product_output_matrix, preferred_element_type=jnp.float32)
    opm_update = lax.map(opm_row, (jnp.transpose(outer_factors[0], (1, 0, 2)), pair_count))
    pairwise_out = (pairwise.astype(jnp.float32) + tri_update + opm_update).astype(jnp.bfloat16)
    return (refreshed_lineup_state, pairwise_out)
```

```python
import math

import jax
import jax.numpy as jnp
from jax import lax
from jax.sharding import PartitionSpec as P

PER_FOCUS_DIM = 32


def layer_normalize(values):
    values = values.astype(jnp.float32)
    center = values - jnp.mean(values, -1, keepdims=True)
    spread = jnp.mean(center * center, -1, keepdims=True)
    return center * lax.rsqrt(spread + 1e-05)


def soft_weights(attention_scores):
    row_max = jnp.max(attention_scores, -1, keepdims=True)
    shifted = jnp.exp(attention_scores - row_max)
    return (shifted / jnp.sum(shifted, -1, keepdims=True)).astype(jnp.bfloat16)


def span_mask(aligned_residue_bounds, length_value):
    places = jnp.arange(length_value, dtype=jnp.int32)
    inside = (places[None, :] >= aligned_residue_bounds[:, 0:1]) & (
        places[None, :] < aligned_residue_bounds[:, 1:2]
    )
    return inside.astype(jnp.float32)


def gather_head(value, axis):
    if lax.axis_size("head") != 2:
        return lax.all_gather(value, "head", axis=axis, tiled=True)
    other = lax.ppermute(value, "head", [(0, 1), (1, 0)])
    first = lax.axis_index("head") == 0
    return jnp.concatenate(
        [jnp.where(first, value, other), jnp.where(first, other, value)], axis=axis
    )


def sum_to_owner(partial_value):
    count = lax.axis_size("head")
    width = partial_value.shape[-1] // count
    if count != 2:
        return lax.psum_scatter(
            partial_value.astype(jnp.bfloat16),
            "head",
            scatter_dimension=partial_value.ndim - 1,
            tiled=True,
        ).astype(jnp.float32)
    first = lax.axis_index("head") == 0
    low, high = partial_value[..., :width], partial_value[..., width:]
    sent = jnp.where(first, high, low).astype(jnp.bfloat16)
    got = lax.ppermute(sent, "head", [(0, 1), (1, 0)])
    return jnp.where(first, low, high) + got.astype(jnp.float32)


def local(
    lineup_state,
    pairwise,
    aligned_residue_bounds,
    residue_valid_mask,
    coupling_offset_weight_map,
    triangle_bias_matrix,
    alignment_projection_matrix,
    lineup_readout_weight,
    feedfwd_entry_weight,
    feedfwd_exit_weight,
    pair_projection_matrix,
    pair_output_matrix,
    left_right_maps,
    outer_product_output_matrix,
):
    seqs, length, channels = lineup_state.shape
    rows = pairwise.shape[0]
    heads = coupling_offset_weight_map.shape[1]
    pair_heads = triangle_bias_matrix.shape[1]
    depth = left_right_maps.shape[2]
    chips = lax.axis_size("rows")
    cores = lax.axis_size("branch")
    inv_scale = 1.0 / math.sqrt(PER_FOCUS_DIM)
    row_place = lax.axis_index(("rows", "branch"))
    head_location = lax.axis_index("head")
    mask_full = span_mask(aligned_residue_bounds, length)
    mask_own = lax.dynamic_slice_in_dim(mask_full, row_place * seqs, seqs, 0)
    key_valid = residue_valid_mask > 0
    alignment_normed = layer_normalize(lineup_state).astype(jnp.bfloat16)
    pair_normed = layer_normalize(pairwise).astype(jnp.bfloat16)
    bias_matrix = jnp.concatenate([coupling_offset_weight_map, triangle_bias_matrix], axis=1)
    bias_local = jnp.einsum(
        "tue,el->ltu", pair_normed, bias_matrix, preferred_element_type=jnp.float32
    ).astype(jnp.bfloat16)
    factors = jnp.einsum(
        "juf,bfn->bjun", alignment_normed, left_right_maps, preferred_element_type=jnp.float32
    )
    factors = (factors * mask_own[None, :, :, None]).astype(jnp.bfloat16)

    block = cores * rows
    left = jnp.transpose(factors[0].reshape(seqs, chips, block, depth), (1, 0, 2, 3))
    bias_size = bias_local.size
    right_size = seqs * length * depth
    copied = jnp.concatenate([bias_local.reshape(-1), factors[1].reshape(-1)])
    payload = jnp.concatenate(
        [
            jnp.broadcast_to(copied[None], (chips, bias_size + right_size)),
            left.reshape(chips, -1),
        ],
        axis=1,
    )
    payload = payload.reshape(chips, -1, 128)
    got = lax.all_to_all(payload, "rows", 0, 0, tiled=True)
    got = lax.all_gather(got, "branch", axis=1)
    got = got.reshape(chips, cores, -1)
    bias = jnp.transpose(
        got[:, :, :bias_size].reshape(chips, cores, heads + pair_heads, rows, length),
        (2, 0, 1, 3, 4),
    ).reshape(heads + pair_heads, length, length)
    right_all = got[:, :, bias_size : bias_size + right_size].reshape(-1, length, depth)
    left_all = got[:, :, bias_size + right_size :].reshape(-1, cores, rows, depth)
    left_own = lax.dynamic_index_in_dim(left_all, lax.axis_index("branch"), 1, keepdims=False)

    lineup_mapped = jnp.einsum(
        "tvf,xfp->xtvp",
        alignment_normed,
        alignment_projection_matrix,
        preferred_element_type=jnp.float32,
    )
    qkv = lineup_mapped[:3].astype(jnp.bfloat16).reshape(3, seqs, length, heads, PER_FOCUS_DIM)
    alignment_gate = jax.nn.sigmoid(lineup_mapped[3])
    pair_proj = jnp.einsum(
        "ijc,gcd->gijd", pair_normed, pair_projection_matrix, preferred_element_type=jnp.float32
    )
    pair_qkv = pair_proj[:3].astype(jnp.bfloat16)
    pair_qkv = pair_qkv.reshape(3, rows, length, pair_heads, PER_FOCUS_DIM)
    pair_gate = jax.nn.sigmoid(pair_proj[3])

    scores = inv_scale * jnp.einsum(
        "xtza,xfza->xztf", qkv[0], qkv[1], preferred_element_type=jnp.float32
    )
    scores = scores + bias[:heads].astype(jnp.float32)[None]
    scores = jnp.where(mask_own[:, None, None, :] > 0, scores, -1000000000.0)
    mixed = jnp.einsum(
        "fxkc,fcxz->fkxz", soft_weights(scores), qkv[2], preferred_element_type=jnp.float32
    ).reshape(seqs, length, heads * PER_FOCUS_DIM)
    mixed = gather_head((mixed * alignment_gate).astype(jnp.bfloat16), 2)

    tri_scores = inv_scale * jnp.einsum(
        "ijhd,ikhd->ihjk", pair_qkv[0], pair_qkv[1], preferred_element_type=jnp.float32
    )
    tri_scores = tri_scores + bias[heads:].astype(jnp.float32)[None]
    tri_scores = jnp.where(key_valid[None, None, None, :], tri_scores, -1000000000.0)
    pair_mixed = jnp.einsum(
        "ihjk,ikhd->ijhd",
        soft_weights(tri_scores),
        pair_qkv[2],
        preferred_element_type=jnp.float32,
    ).reshape(rows, length, pair_heads * PER_FOCUS_DIM)
    pair_mixed = gather_head((pair_mixed * pair_gate).astype(jnp.bfloat16), 2)

    blended = lineup_state.astype(jnp.float32) + jnp.dot(
        mixed.reshape(seqs * length, -1),
        lineup_readout_weight,
        preferred_element_type=jnp.float32,
    ).reshape(seqs, length, channels)
    standardized = layer_normalize(blended).astype(jnp.bfloat16)
    hidden = jax.nn.relu(
        jnp.einsum(
            "src,cf->srf", standardized, feedfwd_entry_weight, preferred_element_type=jnp.float32
        )
    ).astype(jnp.bfloat16)
    partial_value = jnp.einsum(
        "srf,fc->src", hidden, feedfwd_exit_weight, preferred_element_type=jnp.float32
    )
    summed = sum_to_owner(partial_value)
    own_width = channels // lax.axis_size("head")
    owned = lax.dynamic_slice_in_dim(blended, head_location * own_width, own_width, 2)
    refreshed = (owned + summed).astype(jnp.bfloat16)

    mask_rows = lax.dynamic_slice_in_dim(mask_full, row_place * rows, rows, 1)
    pair_count = jnp.dot(mask_rows.T, mask_full, precision=lax.Precision.HIGHEST)
    col_block = math.gcd(length, 128)

    def outer_block(col_start):
        cols = lax.dynamic_slice_in_dim(right_all, col_start, col_block, 1)
        outer_sum = lax.dot_general(
            left_own, cols, (((0,), (0,)), ((), ())), preferred_element_type=jnp.float32
        )
        counts = lax.dynamic_slice_in_dim(pair_count, col_start, col_block, 1)
        outer_mean = (outer_sum / counts[:, None, :, None]).astype(jnp.bfloat16)
        outer_mean = jnp.transpose(outer_mean, (0, 2, 1, 3)).reshape(rows * col_block, -1)
        return jnp.dot(
            outer_mean, outer_product_output_matrix, preferred_element_type=jnp.float32
        ).reshape(rows, col_block, -1)

    starts = jnp.arange(length // col_block, dtype=jnp.int32) * col_block
    opm_update = jnp.transpose(lax.map(outer_block, starts), (1, 0, 2, 3))
    opm_update = opm_update.reshape(rows, length, -1)
    width_z = pair_output_matrix.shape[1]
    tri_update = jnp.dot(
        pair_mixed.reshape(rows * length, -1),
        pair_output_matrix,
        preferred_element_type=jnp.float32,
    ).reshape(rows, length, width_z)
    pair_own = lax.dynamic_slice_in_dim(pairwise, head_location * width_z, width_z, 2)
    pairwise_out = (pair_own.astype(jnp.float32) + tri_update + opm_update).astype(jnp.bfloat16)
    return (refreshed, pairwise_out)


def solution(mesh):
    in_specs = (
        P(("parts", "rows", "branch"), None, None),
        P(("parts", "rows", "branch"), None, None),
        P("parts", None),
        P("parts"),
        P(None, "head"),
        P(None, "head"),
        P(None, None, "head"),
        P(),
        P(None, "head"),
        P("head", None),
        P(None, None, "head"),
        P(None, "head"),
        P(),
        P(None, "head"),
    )
    out_specs = (
        P(("parts", "rows", "branch"), None, "head"),
        P(("parts", "rows", "branch"), None, "head"),
    )
    return jax.shard_map(local, mesh=mesh, in_specs=in_specs, out_specs=out_specs, check_vma=False)
```

```python
import functools
import math

import jax
import jax.numpy as jnp
from jax import lax
from jax.experimental import pallas as pl
from jax.experimental.pallas import tpu as pltpu
from jax.sharding import PartitionSpec as P


PER_FOCUS_DIM = 32
F32 = jnp.float32
BF16 = jnp.bfloat16
LOG2E = math.log2(math.e)
SCALE = LOG2E / math.sqrt(PER_FOCUS_DIM)
FAR = -1.0e30

VMEM = pl.BlockSpec(memory_space=pltpu.VMEM)
HBM = pl.BlockSpec(memory_space=pltpu.HBM)


def nt(a, b):
    return lax.dot_general(a, b, (((1,), (1,)), ((), ())), preferred_element_type=F32)


def nn(a, b):
    return lax.dot_general(a, b, (((1,), (0,)), ((), ())), preferred_element_type=F32)


def normed(values):
    values = values.astype(F32)
    center = values - jnp.mean(values, -1, keepdims=True)
    spread = jnp.mean(center * center, -1, keepdims=True)
    return center * lax.rsqrt(spread + 1e-05)


def places(shape, axis):
    return lax.broadcasted_iota(jnp.int32, shape, axis)


def place_of(cores):
    return lax.axis_index("rows") * cores + lax.axis_index("branch")


def span_of(bounds_ref, which):
    bounds = bounds_ref[...].astype(F32)
    kept = jnp.where(places(bounds.shape, 1) == which, bounds, 0.0)
    span = jnp.sum(kept, axis=1, keepdims=True)
    return span[0:1], span[1:2]


def within(at, begin, end):
    at = at.astype(F32)
    return (at >= begin) & (at < end)


def fetch(pairs, sem):
    copies = [pltpu.make_async_copy(a, b, sem.at[j]) for j, (a, b) in enumerate(pairs)]
    for copy in copies:
        copy.start()
    return copies


def pre_kernel(cores, *refs):
    pay_ref, sem = refs[6], refs[13]
    copies = fetch(list(zip(refs[:6], refs[7:13])), sem)
    x_ref, p_ref, mb_ref, tb_ref, lr_ref, bounds_ref = refs[7:13]
    seqs, length, _ = x_ref.shape
    rows = p_ref.shape[0]
    chips = pay_ref.shape[0]
    for copy in copies:
        copy.wait()
    bias_w = jnp.concatenate([mb_ref[...].astype(F32), tb_ref[...].astype(F32)], axis=0)
    bias_w = bias_w.astype(BF16)
    heads = bias_w.shape[0]
    depth = lr_ref.shape[1]
    first_seq = place_of(cores) * seqs
    pieces = []
    biases = []
    for i in range(rows):
        pn = normed(p_ref[i]).astype(BF16)
        biases.append(nt(bias_w, pn))
    for h in range(heads):
        pieces.append(jnp.concatenate([b[h : h + 1] for b in biases], axis=0))
    left = None
    zero = jnp.zeros(lr_ref.shape[1:], BF16)
    for s in range(seqs):
        xn = normed(x_ref[s]).astype(BF16)
        begin, end = span_of(bounds_ref, first_seq + s)
        seen = within(places((1, length), 1), begin, end)
        pieces.append(nt(lr_ref[1], xn) * seen.astype(F32))
        weight = jnp.concatenate(
            [lr_ref[0] if other == s else zero for _ in range(cores) for other in range(seqs)],
            axis=0,
        )
        term = nt(xn, weight) * within(places((length, 1), 0), begin, end).astype(F32)
        left = term if left is None else left + term
    width = left.shape[1]
    group = places((rows, width), 1) // (seqs * depth)
    copied = jnp.concatenate(pieces, axis=0).astype(BF16)
    count = copied.shape[0]
    for d in range(chips):
        pay_ref[d, 0:count, :] = copied
        mine = left[d * cores * rows : d * cores * rows + rows]
        for c in range(1, cores):
            begin = (d * cores + c) * rows
            mine = jnp.where(group == c, left[begin : begin + rows], mine)
        if width < length:
            mine = jnp.concatenate([mine, jnp.zeros((rows, length - width), F32)], axis=1)
        pay_ref[d, count : count + rows, :] = mine.astype(BF16)


def proj_kernel(heads, pair_heads, *refs):
    count = 5
    sm_ref, v_ref, g_ref, st_ref, pv_ref, pg_ref, own_ref, lay_ref = refs[count : count + 8]
    held = refs[count + 8 : 2 * count + 8]
    turn_ref, rows_ref, sem = refs[2 * count + 8 :]
    copies = fetch(list(zip(refs[:count], held)), sem)
    x_ref, p_ref, aw_ref, pw_ref, ow_ref = held
    seqs, _, _ = x_ref.shape
    rows = p_ref.shape[0]
    for copy in copies:
        copy.wait()
    for s in range(seqs):
        xn = normed(x_ref[s]).astype(BF16)
        q = nn(xn, aw_ref[0]).astype(BF16)
        k = nn(xn, aw_ref[1]).astype(BF16)
        v_ref[s] = nn(xn, aw_ref[2]).astype(BF16)
        g_ref[s] = jax.nn.sigmoid(nn(xn, aw_ref[3]))
        head = places(q.shape, 1) // PER_FOCUS_DIM
        for h in range(heads):
            sm_ref[s, h] = nt(jnp.where(head == h, q, jnp.zeros_like(q)), k) * SCALE
    qv = jnp.concatenate([pw_ref[0], pw_ref[2]], axis=0)
    kg = jnp.concatenate([pw_ref[1], pw_ref[3]], axis=0)
    width = own_ref.shape[1]
    begin = pl.multiple_of(lax.axis_index("head") * width, width)
    for i in range(rows):
        pn = normed(p_ref[i]).astype(BF16)
        first = nt(pn, qv).astype(BF16)
        second = nt(pn, kg)
        pv_ref[i] = first
        pg_ref[i] = jax.nn.sigmoid(second)
        second = second.astype(BF16)
        head = places(first.shape, 1) // PER_FOCUS_DIM
        for h in range(pair_heads):
            st_ref[i, h] = nt(jnp.where(head == h, first, jnp.zeros_like(first)), second) * SCALE
        turn_ref[...] = p_ref[i].astype(F32).T
        own_ref[i] = turn_ref[pl.ds(begin, width), :].astype(BF16)
    groups = 128 // width
    steps = lay_ref.shape[1] // 128
    depth = steps * groups
    turned = ow_ref[...].astype(F32)
    rows_ref[...] = jnp.concatenate([turned] * groups, axis=0).T
    group = places((depth, 128), 1) // width
    for step in range(steps):
        tile = rows_ref[pl.ds(step, depth, stride=depth), :]
        for g in range(1, groups):
            part = rows_ref[pl.ds(g * steps + step, depth, stride=depth), :]
            tile = jnp.where(group == g, part, tile)
        lay_ref[:, step * 128 : (step + 1) * 128] = tile.astype(BF16)


def gather_bias(bias_ref, mine_ref, other_ref, first, heads, rows, cores):
    chips = mine_ref.shape[0]
    core = lax.axis_index("branch")
    for d in range(chips):
        for ref, c in ((mine_ref, core), (other_ref, 1 - core)):
            begin = pl.multiple_of((d * cores + c) * rows, rows)
            block = ref[d, first * rows : (first + heads) * rows, :].astype(F32) * LOG2E
            for h in range(heads):
                bias_ref[h, pl.ds(begin, rows), :] = block[h * rows : (h + 1) * rows]


def attend(scores, values, gate, offset):
    width = values.shape[1]
    head = (places(values.shape, 1) - offset) // PER_FOCUS_DIM
    inside = places(values.shape, 1) >= offset
    mixed = total = None
    for h, score in enumerate(scores):
        top = jnp.max(score, axis=-1, keepdims=True)
        weights = jnp.exp2(score - top).astype(BF16)
        here = (head == h) & inside
        value = jnp.where(here, values, jnp.zeros_like(values))
        ones = jnp.where(here, jnp.ones_like(values), jnp.zeros_like(values))
        if width % 128 == 0:
            both = nn(weights, jnp.concatenate([value, ones], axis=1))
            part, norm = both[:, :width], both[:, width:]
        else:
            part, norm = nn(weights, value), nn(weights, ones)
        mixed = part if mixed is None else mixed + part
        total = norm if total is None else total + norm
    return gate * mixed / jnp.where(total > 0, total, 1.0)


def align_kernel(cores, rows, mine_ref, other_ref, sm_ref, v_ref, g_ref, bounds_ref, out_ref, bias_ref):
    seqs, heads, length, _ = sm_ref.shape
    gather_bias(bias_ref, mine_ref, other_ref, 0, heads, rows, cores)
    first_seq = place_of(cores) * seqs
    for s in range(seqs):
        begin, end = span_of(bounds_ref, first_seq + s)
        seen = within(places((1, length), 1), begin, end)
        scores = [jnp.where(seen, sm_ref[s, h] + bias_ref[h], FAR) for h in range(heads)]
        out_ref[s] = attend(scores, v_ref[s], g_ref[s], 0).astype(BF16)


def tri_kernel(cores, first, mine_ref, other_ref, st_ref, v_ref, g_ref, valid_ref, out_ref, bias_ref):
    rows, heads, _, _ = st_ref.shape
    offset = heads * PER_FOCUS_DIM
    gather_bias(bias_ref, mine_ref, other_ref, first, heads, rows, cores)
    seen = valid_ref[...] > 0
    for h in range(heads):
        bias_ref[h] = jnp.where(seen, bias_ref[h], FAR)
    for i in range(rows):
        scores = [st_ref[i, h] + bias_ref[h] for h in range(heads)]
        out = attend(scores, v_ref[i], g_ref[i], offset)
        out_ref[i] = out.T[offset : 2 * offset].astype(BF16)


def transition_kernel(parts, *refs):
    heads_refs = refs[:parts]
    x_ref, wo_ref, entry_ref, exit_ref = refs[parts : parts + 4]
    own_ref, sent_ref = refs[parts + 4 :]
    seqs = x_ref.shape[0]
    features = heads_refs[0].shape[2]
    here = lax.axis_index("head")
    for s in range(seqs):
        blended = x_ref[s].astype(F32)
        for j in range(parts):
            which = jnp.where(j == 0, here, 1 - here) if parts == 2 else j
            begin = pl.multiple_of(which * features, features)
            blended = blended + nn(heads_refs[j][s], wo_ref[pl.ds(begin, features), :])
        hidden = jnp.maximum(nn(normed(blended).astype(BF16), entry_ref[...]), 0.0).astype(BF16)
        partial = nn(hidden, exit_ref[...])
        if parts == 2:
            half = partial.shape[1] // 2
            own = here == 0
            kept = jnp.where(own, partial[:, :half], partial[:, half:])
            base = jnp.where(own, blended[:, :half], blended[:, half:])
            own_ref[s] = base + kept
            sent_ref[s] = jnp.where(own, partial[:, half:], partial[:, :half]).astype(BF16)
        else:
            own_ref[s] = blended
            sent_ref[s] = partial.astype(BF16)


def outer_kernel(cores, seqs, heads, mine_ref, other_ref, w_ref, bounds_ref, own_ref, out_ref, a_ref, b_ref):
    rows, width, length = out_ref.shape
    chips = mine_ref.shape[0]
    depth = w_ref.shape[0]
    lanes = depth * cores * seqs
    groups = 128 // width
    steps = depth // groups
    total = chips * cores * seqs
    core = lax.axis_index("branch")
    first = heads * rows
    lane_group = places((rows, lanes), 1) // depth
    for d in range(chips):
        for which, ref in enumerate((mine_ref, other_ref)):
            block = ref[d, first : first + seqs * depth, :].astype(F32)
            left = ref[d, first + seqs * depth : first + seqs * depth + rows, :lanes].astype(F32)
            for s in range(seqs):
                row = (d * cores + which) * seqs + s
                for g in range(groups):
                    begin = s * depth + g * steps
                    for t in range(length // 128):
                        piece = block[begin : begin + steps, t * 128 : (t + 1) * 128]
                        b_ref[g, t, pl.ds(row, steps, stride=total), :] = piece
                kept = jnp.where(lane_group == core * seqs + s, left, 0.0)
                a_ref[pl.ds(row, rows, stride=total), :] = kept
    a = a_ref[...].astype(BF16)
    begin, end = bounds_ref[0:1].astype(F32), bounds_ref[1:2].astype(F32)
    whole = within(places((length, 1), 0), begin, end).astype(BF16)
    owned = within(places((rows, 1), 0) + place_of(cores) * rows, begin, end).astype(BF16)
    count = nt(owned, whole)
    share = 1.0 / count
    gathered = [[] for _ in range(rows)]
    for step in range(steps):
        tile = jnp.concatenate([w_ref[:, step * 128 : (step + 1) * 128]] * (cores * seqs), axis=0)
        g = nn(a, tile).astype(BF16)
        for i in range(rows):
            gathered[i].append(g[i * total : (i + 1) * total])
    b = [[b_ref[g, t].T.astype(BF16) for t in range(length // 128)] for g in range(groups)]
    for i in range(rows):
        g = jnp.concatenate(gathered[i], axis=0)
        for t in range(length // 128):
            acc = None
            for k in range(groups):
                part = nn(b[k][t], g).T[k * width : (k + 1) * width]
                acc = part if acc is None else acc + part
            at = slice(t * 128, (t + 1) * 128)
            out_ref[i, :, at] = acc * share[i : i + 1, at] + own_ref[i, :, at].astype(F32)


def close_kernel(parts, *refs):
    heads_refs = refs[:parts]
    opm_ref, w_ref, base_ref, sum_ref, out_ref, new_ref = refs[parts:]
    new_ref[...] = (base_ref[...] + sum_ref[...].astype(F32)).astype(BF16)
    rows = opm_ref.shape[0]
    features = heads_refs[0].shape[1]
    own = lax.axis_index("head") == 0
    weights = [w_ref[:, j * features : (j + 1) * features].astype(F32) for j in range(parts)]
    if parts == 2:
        weights = [jnp.where(own, weights[0], weights[1]), jnp.where(own, weights[1], weights[0])]
    weights = [w.astype(BF16) for w in weights]
    for i in range(rows):
        out = opm_ref[i]
        for j in range(parts):
            out = out + nn(weights[j], heads_refs[j][i])
        out_ref[i] = out.astype(BF16)


def call(kernel, ins, outs, scratch=(), left=(), flops=0):
    size = sum(a.size * a.dtype.itemsize for a in ins) + sum(
        math.prod(s) * jnp.dtype(d).itemsize for s, d in outs
    )
    held = sum(a.inner_aval.size * 4 for a in scratch)
    limit = min(max((size + held) * 2, 8 << 20), 60 << 20)
    return pl.pallas_call(
        kernel,
        compiler_params=pltpu.CompilerParams(vmem_limit_bytes=limit),
        out_shape=tuple(jax.ShapeDtypeStruct(s, d) for s, d in outs),
        in_specs=[HBM if i in left else VMEM for i in range(len(ins))],
        out_specs=tuple(VMEM for _ in outs),
        scratch_shapes=list(scratch),
        cost_estimate=pl.CostEstimate(flops=flops, bytes_accessed=size, transcendentals=0),
    )(*ins)


def held_copies(arrays):
    return [*(pltpu.VMEM(a.shape, a.dtype) for a in arrays), pltpu.SemaphoreType.DMA((len(arrays),))]


def from_heads(value):
    if lax.axis_size("head") == 2:
        return [value, lax.ppermute(value, "head", [(0, 1), (1, 0)])]
    every = lax.all_gather(value, "head", axis=0)
    return [every[j] for j in range(every.shape[0])]


def local(
    lineup_state,
    pairwise,
    aligned_residue_bounds,
    residue_valid_mask,
    coupling_offset_weight_map,
    triangle_bias_matrix,
    alignment_projection_matrix,
    lineup_readout_weight,
    feedfwd_entry_weight,
    feedfwd_exit_weight,
    pair_projection_matrix,
    pair_output_matrix,
    left_right_maps,
    outer_product_output_matrix,
):
    seqs, length, channels = lineup_state.shape
    rows, _, pair_channels = pairwise.shape
    heads = coupling_offset_weight_map.shape[1]
    pair_heads = triangle_bias_matrix.shape[1]
    every_head = heads + pair_heads
    depth = left_right_maps.shape[2]
    chips = lax.axis_size("rows")
    cores = lax.axis_size("branch")
    parts = lax.axis_size("head")
    width = outer_product_output_matrix.shape[1]
    features = heads * PER_FOCUS_DIM
    pair_features = pair_heads * PER_FOCUS_DIM
    total = chips * cores * seqs
    bounds = aligned_residue_bounds.T

    first = (
        lineup_state,
        pairwise,
        coupling_offset_weight_map.T,
        triangle_bias_matrix.T,
        jnp.swapaxes(left_right_maps, 1, 2),
        bounds,
    )
    (payload,) = call(
        functools.partial(pre_kernel, cores),
        first,
        (((chips, every_head * rows + seqs * depth + rows, length), BF16),),
        scratch=held_copies(first),
        left=range(len(first)),
    )
    mine = lax.all_to_all(payload, "rows", 0, 0, tiled=True)
    other = lax.ppermute(mine, "branch", [(0, 1), (1, 0)])

    groups = 128 // width
    second = (
        lineup_state,
        pairwise,
        alignment_projection_matrix,
        jnp.swapaxes(pair_projection_matrix, 1, 2),
        outer_product_output_matrix.T,
    )
    scores, values, gate, tri_scores, tri_values, tri_gate, own_pair, outer_w = call(
        functools.partial(proj_kernel, heads, pair_heads),
        second,
        (
            ((seqs, heads, length, length), F32),
            ((seqs, length, features), BF16),
            ((seqs, length, features), F32),
            ((rows, pair_heads, length, length), F32),
            ((rows, length, 2 * pair_features), BF16),
            ((rows, length, 2 * pair_features), F32),
            ((rows, width, length), BF16),
            ((depth, depth * width), BF16),
        ),
        scratch=[
            *held_copies(second)[:-1],
            pltpu.VMEM((pair_channels, length), F32),
            pltpu.VMEM((depth * depth, 128), F32),
            held_copies(second)[-1],
        ],
        left=range(len(second)),
        flops=1 << 28,
    )

    (mixed,) = call(
        functools.partial(align_kernel, cores, rows),
        (mine, other, scores, values, gate, bounds),
        (((seqs, length, features), BF16),),
        scratch=[pltpu.VMEM((heads, length, length), F32)],
        flops=1 << 28,
    )
    mixed = from_heads(mixed)
    (pair_mixed,) = call(
        functools.partial(tri_kernel, cores, heads),
        (mine, other, tri_scores, tri_values, tri_gate, residue_valid_mask.reshape(1, -1)),
        (((rows, pair_features, length), BF16),),
        scratch=[pltpu.VMEM((pair_heads, length, length), F32)],
        flops=1 << 28,
    )
    pair_mixed = from_heads(pair_mixed)

    out_channels = channels // 2 if parts == 2 else channels
    owned, partial = call(
        functools.partial(transition_kernel, parts),
        (*mixed, lineup_state, lineup_readout_weight, feedfwd_entry_weight, feedfwd_exit_weight),
        (((seqs, length, out_channels), F32), ((seqs, length, out_channels), BF16)),
        flops=1 << 28,
    )
    if parts == 2:
        received = lax.ppermute(partial, "head", [(0, 1), (1, 0)])
    else:
        own_width = channels // parts
        received = lax.psum_scatter(partial, "head", scatter_dimension=2, tiled=True)
        owned = lax.dynamic_slice_in_dim(owned, lax.axis_index("head") * own_width, own_width, 2)

    (opm,) = call(
        functools.partial(outer_kernel, cores, seqs, every_head),
        (mine, other, outer_w, bounds, own_pair),
        (((rows, width, length), F32),),
        scratch=[
            pltpu.VMEM((rows * total, depth * cores * seqs), F32),
            pltpu.VMEM((groups, length // 128, depth // groups * total, 128), F32),
        ],
        flops=1 << 28,
    )
    pair_out, refreshed = call(
        functools.partial(close_kernel, parts),
        (*pair_mixed, opm, pair_output_matrix.T, owned, received),
        (((rows, width, length), BF16), (owned.shape, BF16)),
        flops=1 << 26,
    )
    return (refreshed, jnp.swapaxes(pair_out, 1, 2))


def solution(mesh):
    in_specs = (
        P(("parts", "rows", "branch"), None, None),
        P(("parts", "rows", "branch"), None, None),
        P("parts", None),
        P("parts"),
        P(None, "head"),
        P(None, "head"),
        P(None, None, "head"),
        P(),
        P(None, "head"),
        P("head", None),
        P(None, None, "head"),
        P(None, "head"),
        P(),
        P(None, "head"),
    )
    out_specs = (
        P(("parts", "rows", "branch"), None, "head"),
        P(("parts", "rows", "branch"), None, "head"),
    )


    return jax.shard_map(local, mesh=mesh, in_specs=in_specs, out_specs=out_specs, check_vma=False)
```

```python
import functools
import math

import jax
import jax.numpy as jnp
from jax import lax
from jax.experimental import pallas as pl
from jax.experimental.pallas import tpu as pltpu
from jax.sharding import PartitionSpec as P


PER_FOCUS_DIM = 32
F32 = jnp.float32
BF16 = jnp.bfloat16
LOG2E = math.log2(math.e)
SCALE = LOG2E / math.sqrt(PER_FOCUS_DIM)
FAR = -1.0e30

VMEM = pl.BlockSpec(memory_space=pltpu.VMEM)
HBM = pl.BlockSpec(memory_space=pltpu.HBM)


def nt(a, b):
    return lax.dot_general(a, b, (((1,), (1,)), ((), ())), preferred_element_type=F32)


def nn(a, b):
    return lax.dot_general(a, b, (((1,), (0,)), ((), ())), preferred_element_type=F32)


def normed(values):
    values = values.astype(F32)
    center = values - jnp.mean(values, -1, keepdims=True)
    spread = jnp.mean(center * center, -1, keepdims=True)
    return center * lax.rsqrt(spread + 1e-05)


def places(shape, axis):
    return lax.broadcasted_iota(jnp.int32, shape, axis)


def place_of(cores):
    return lax.axis_index("rows") * cores + lax.axis_index("branch")


def span_of(bounds_ref, which):
    bounds = bounds_ref[...].astype(F32)
    kept = jnp.where(places(bounds.shape, 1) == which, bounds, 0.0)
    span = jnp.sum(kept, axis=1, keepdims=True)
    return span[0:1], span[1:2]


def within(at, begin, end):
    at = at.astype(F32)
    return (at >= begin) & (at < end)


def fetch(pairs, sem):
    copies = [pltpu.make_async_copy(a, b, sem.at[j]) for j, (a, b) in enumerate(pairs)]
    for copy in copies:
        copy.start()
    return copies


def pre_kernel(cores, *refs):
    pay_ref, sem = refs[6], refs[13]
    copies = fetch(list(zip(refs[:6], refs[7:13])), sem)
    x_ref, p_ref, mb_ref, tb_ref, lr_ref, bounds_ref = refs[7:13]
    seqs, length, _ = x_ref.shape
    rows = p_ref.shape[0]
    chips = pay_ref.shape[0]
    for copy in copies:
        copy.wait()
    bias_w = jnp.concatenate([mb_ref[...].astype(F32), tb_ref[...].astype(F32)], axis=0)
    bias_w = bias_w.astype(BF16)
    heads = bias_w.shape[0]
    depth = lr_ref.shape[1]
    first_seq = place_of(cores) * seqs
    pieces = []
    biases = []
    for i in range(rows):
        pn = normed(p_ref[i]).astype(BF16)
        biases.append(nt(bias_w, pn))
    for h in range(heads):
        pieces.append(jnp.concatenate([b[h : h + 1] for b in biases], axis=0))
    left = None
    zero = jnp.zeros(lr_ref.shape[1:], BF16)
    for s in range(seqs):
        xn = normed(x_ref[s]).astype(BF16)
        begin, end = span_of(bounds_ref, first_seq + s)
        seen = within(places((1, length), 1), begin, end)
        pieces.append(nt(lr_ref[1], xn) * seen.astype(F32))
        weight = jnp.concatenate(
            [lr_ref[0] if other == s else zero for _ in range(cores) for other in range(seqs)],
            axis=0,
        )
        term = nt(xn, weight) * within(places((length, 1), 0), begin, end).astype(F32)
        left = term if left is None else left + term
    width = left.shape[1]
    group = places((rows, width), 1) // (seqs * depth)
    copied = jnp.concatenate(pieces, axis=0).astype(BF16)
    count = copied.shape[0]
    for d in range(chips):
        pay_ref[d, 0:count, :] = copied
        mine = left[d * cores * rows : d * cores * rows + rows]
        for c in range(1, cores):
            begin = (d * cores + c) * rows
            mine = jnp.where(group == c, left[begin : begin + rows], mine)
        if width < length:
            mine = jnp.concatenate([mine, jnp.zeros((rows, length - width), F32)], axis=1)
        pay_ref[d, count : count + rows, :] = mine.astype(BF16)


def proj_kernel(cores, heads, pair_heads, *refs):
    count = 7
    sm_ref, v_ref, g_ref, st_ref, pv_ref, pg_ref, own_ref, lay_ref, mask_ref, share_ref = refs[
        count : count + 10
    ]
    held = refs[count + 10 : 2 * count + 10]
    turn_ref, rows_ref, sem = refs[2 * count + 10 :]
    copies = fetch(list(zip(refs[:count], held)), sem)
    x_ref, p_ref, aw_ref, pw_ref, ow_ref, bounds_ref, valid_ref = held
    seqs, length, _ = x_ref.shape
    rows = p_ref.shape[0]
    for copy in copies:
        copy.wait()
    first_seq = place_of(cores) * seqs
    for s in range(seqs):
        begin, end = span_of(bounds_ref, first_seq + s)
        mask_ref[s : s + 1] = jnp.where(within(places((1, length), 1), begin, end), 0.0, FAR)
    mask_ref[seqs : seqs + 1] = jnp.where(valid_ref[...] > 0, 0.0, FAR)
    begin, end = bounds_ref[0:1].astype(F32), bounds_ref[1:2].astype(F32)
    whole = within(places((length, 1), 0), begin, end).astype(BF16)
    owned = within(places((rows, 1), 0) + place_of(cores) * rows, begin, end).astype(BF16)
    share_ref[...] = 1.0 / nt(owned, whole)
    for s in range(seqs):
        xn = normed(x_ref[s]).astype(BF16)
        q = nn(xn, aw_ref[0]).astype(BF16)
        k = nn(xn, aw_ref[1]).astype(BF16)
        v_ref[s] = nn(xn, aw_ref[2]).astype(BF16)
        g_ref[s] = jax.nn.sigmoid(nn(xn, aw_ref[3]))
        head = places(q.shape, 1) // PER_FOCUS_DIM
        for h in range(heads):
            sm_ref[s, h] = nt(jnp.where(head == h, q, jnp.zeros_like(q)), k) * SCALE
    width = own_ref.shape[1]
    begin = pl.multiple_of(lax.axis_index("head") * width, width)
    for i in range(rows):
        pn = normed(p_ref[i]).astype(BF16)
        q = nt(pn, pw_ref[0]).astype(BF16)
        k = nt(pn, pw_ref[1]).astype(BF16)
        pv_ref[i] = nt(pw_ref[2], pn).astype(BF16)
        pg_ref[i] = jax.nn.sigmoid(nt(pw_ref[3], pn))
        head = places(q.shape, 1) // PER_FOCUS_DIM
        for h in range(pair_heads):
            st_ref[i, h] = nt(jnp.where(head == h, q, jnp.zeros_like(q)), k) * SCALE
        turn_ref[...] = p_ref[i].astype(F32).T
        own_ref[i] = turn_ref[pl.ds(begin, width), :].astype(BF16)
    groups = 128 // width
    steps = lay_ref.shape[1] // 128
    depth = steps * groups
    turned = ow_ref[...].astype(F32)
    rows_ref[...] = jnp.concatenate([turned] * groups, axis=0).T
    group = places((depth, 128), 1) // width
    for step in range(steps):
        tile = rows_ref[pl.ds(step, depth, stride=depth), :]
        for g in range(1, groups):
            part = rows_ref[pl.ds(g * steps + step, depth, stride=depth), :]
            tile = jnp.where(group == g, part, tile)
        lay_ref[:, step * 128 : (step + 1) * 128] = tile.astype(BF16)


def gather_bias(bias_ref, mine_ref, other_ref, first, heads, rows, cores):
    chips = mine_ref.shape[0]
    core = lax.axis_index("branch")
    for d in range(chips):
        for ref, c in ((mine_ref, core), (other_ref, 1 - core)):
            begin = pl.multiple_of((d * cores + c) * rows, rows)
            block = ref[d, first * rows : (first + heads) * rows, :].astype(F32) * LOG2E
            for h in range(heads):
                bias_ref[h, pl.ds(begin, rows), :] = block[h * rows : (h + 1) * rows]


def attend(scores, values, gate):
    width = values.shape[1]
    head = places(values.shape, 1) // PER_FOCUS_DIM
    mixed = total = None
    for h, score in enumerate(scores):
        top = jnp.max(score, axis=-1, keepdims=True)
        weights = jnp.exp2(score - top).astype(BF16)
        here = head == h
        value = jnp.where(here, values, jnp.zeros_like(values))
        ones = jnp.where(here, jnp.ones_like(values), jnp.zeros_like(values))
        if width % 128 == 0:
            both = nn(weights, jnp.concatenate([value, ones], axis=1))
            part, norm = both[:, :width], both[:, width:]
        else:
            part, norm = nn(weights, value), nn(weights, ones)
        mixed = part if mixed is None else mixed + part
        total = norm if total is None else total + norm
    return gate * mixed / total


def align_kernel(cores, rows, mine_ref, other_ref, sm_ref, v_ref, g_ref, mask_ref, out_ref, bias_ref):
    seqs, heads, _, _ = sm_ref.shape
    gather_bias(bias_ref, mine_ref, other_ref, 0, heads, rows, cores)
    for s in range(seqs):
        mask = mask_ref[s : s + 1]
        scores = [sm_ref[s, h] + (bias_ref[h] + mask) for h in range(heads)]
        out_ref[s] = attend(scores, v_ref[s], g_ref[s]).astype(BF16)


def tri_kernel(cores, first, mine_ref, other_ref, st_ref, v_ref, g_ref, mask_ref, out_ref, bias_ref):
    rows, heads, length, _ = st_ref.shape
    gather_bias(bias_ref, mine_ref, other_ref, first, heads, rows, cores)
    last = mask_ref.shape[0] - 1
    for h in range(heads):
        bias_ref[h] = bias_ref[h] + mask_ref[last : last + 1]
    ones = jnp.ones((8, length), BF16)
    for i in range(rows):
        for h in range(heads):
            score = st_ref[i, h] + bias_ref[h]
            top = jnp.max(score, axis=-1, keepdims=True)
            weights = jnp.exp2(score - top).astype(BF16)
            at = slice(h * PER_FOCUS_DIM, (h + 1) * PER_FOCUS_DIM)
            mixed = nt(v_ref[i, at, :], weights)
            total = nt(ones, weights)[0:1]
            out_ref[i, at, :] = (g_ref[i, at, :] * mixed / total).astype(BF16)


def transition_kernel(parts, *refs):
    heads_refs = refs[:parts]
    x_ref, wo_ref = refs[parts : parts + 2]
    entry_refs = refs[parts + 2 : 2 * parts + 2]
    exit_refs = refs[2 * parts + 2 : 3 * parts + 2]
    out_ref, turn_ref = refs[3 * parts + 2 :]
    seqs = x_ref.shape[0]
    features = heads_refs[0].shape[2]
    width = out_ref.shape[2]
    here = lax.axis_index("head")

    def owned(value):
        if parts == 2:
            return jnp.where(here == 0, value[:, :width], value[:, width:])
        turn_ref[...] = value.T
        return turn_ref[pl.ds(pl.multiple_of(here * width, width), width), :].T

    length = x_ref.shape[1]
    for begin_row in range(0, length, 128):
        at = slice(begin_row, begin_row + 128)
        blended = jnp.concatenate([x_ref[s, at, :] for s in range(seqs)], axis=0).astype(F32)
        for j in range(parts):
            which = jnp.where(j == 0, here, 1 - here) if parts == 2 else j
            begin = pl.multiple_of(which * features, features)
            mixed = jnp.concatenate([heads_refs[j][s, at, :] for s in range(seqs)], axis=0)
            blended = blended + nn(mixed, wo_ref[pl.ds(begin, features), :])
        standardized = normed(blended).astype(BF16)
        out = owned(blended)
        for entry_ref, exit_ref in zip(entry_refs, exit_refs):
            hidden = jnp.maximum(nn(standardized, entry_ref[...]), 0.0).astype(BF16)
            out = out + nn(hidden, exit_ref[...])
        for s in range(seqs):
            out_ref[s, at, :] = out[s * 128 : (s + 1) * 128].astype(BF16)


def outer_kernel(cores, seqs, heads, mine_ref, other_ref, w_ref, share_ref, own_ref, out_ref, a_ref, b_ref):
    rows, width, length = out_ref.shape
    chips = mine_ref.shape[0]
    depth = w_ref.shape[0]
    lanes = depth * cores * seqs
    groups = 128 // width
    steps = depth // groups
    total = chips * cores * seqs
    core = lax.axis_index("branch")
    first = heads * rows
    lane_group = places((rows, lanes), 1) // depth
    for d in range(chips):
        for which, ref in enumerate((mine_ref, other_ref)):
            block = ref[d, first : first + seqs * depth, :].astype(F32)
            left = ref[d, first + seqs * depth : first + seqs * depth + rows, :lanes].astype(F32)
            for s in range(seqs):
                row = (d * cores + which) * seqs + s
                for g in range(groups):
                    begin = s * depth + g * steps
                    for t in range(length // 128):
                        piece = block[begin : begin + steps, t * 128 : (t + 1) * 128]
                        b_ref[g, t, pl.ds(row, steps, stride=total), :] = piece
                kept = jnp.where(lane_group == core * seqs + s, left, 0.0)
                a_ref[pl.ds(row, rows, stride=total), :] = kept
    a = a_ref[...].astype(BF16)
    share = share_ref[...]
    gathered = [[] for _ in range(rows)]
    for step in range(steps):
        tile = jnp.concatenate([w_ref[:, step * 128 : (step + 1) * 128]] * (cores * seqs), axis=0)
        g = nn(a, tile).astype(BF16)
        for i in range(rows):
            gathered[i].append(g[i * total : (i + 1) * total])
    b = [[b_ref[g, t].T.astype(BF16) for t in range(length // 128)] for g in range(groups)]
    for i in range(rows):
        g = jnp.concatenate(gathered[i], axis=0)
        for t in range(length // 128):
            acc = None
            for k in range(groups):
                part = nn(b[k][t], g).T[k * width : (k + 1) * width]
                acc = part if acc is None else acc + part
            at = slice(t * 128, (t + 1) * 128)
            out_ref[i, :, at] = acc * share[i : i + 1, at] + own_ref[i, :, at].astype(F32)


def close_kernel(parts, *refs):
    heads_refs = refs[:parts]
    opm_ref, w_ref, out_ref = refs[parts:]
    rows = opm_ref.shape[0]
    features = heads_refs[0].shape[1]
    own = lax.axis_index("head") == 0
    weights = [w_ref[:, j * features : (j + 1) * features] for j in range(parts)]
    weight = w_ref[...]
    if parts == 2:
        turned = jnp.concatenate([weights[1].astype(F32), weights[0].astype(F32)], axis=1)
        weight = jnp.where(own, weight.astype(F32), turned).astype(BF16)
    for i in range(rows):
        every = jnp.concatenate([ref[i] for ref in heads_refs], axis=0)
        out_ref[i] = (opm_ref[i] + nn(weight, every)).astype(BF16)


def call(kernel, ins, outs, scratch=(), left=(), grant=0, flops=0):
    size = sum(a.size * a.dtype.itemsize for a in ins) + sum(
        math.prod(s) * jnp.dtype(d).itemsize for s, d in outs
    )
    held = sum(a.inner_aval.size * 4 for a in scratch)
    limit = grant or min(max((size + held) * 2, 8 << 20), 60 << 20)
    run = pl.pallas_call(
        kernel,
        compiler_params=pltpu.CompilerParams(vmem_limit_bytes=limit),
        out_shape=tuple(jax.ShapeDtypeStruct(s, d) for s, d in outs),
        in_specs=[HBM if i in left else VMEM for i in range(len(ins))],
        out_specs=tuple(VMEM for _ in outs),
        scratch_shapes=list(scratch),
        cost_estimate=pl.CostEstimate(flops=flops, bytes_accessed=size, transcendentals=0),
    )
    ins = [pltpu.with_memory_space_constraint(a, pltpu.HBM) if i in left else a for i, a in enumerate(ins)]
    return run(*ins)


def held_copies(arrays):
    return [*(pltpu.VMEM(a.shape, a.dtype) for a in arrays), pltpu.SemaphoreType.DMA((len(arrays),))]


def from_heads(value):
    if lax.axis_size("head") == 2:
        return [value, lax.ppermute(value, "head", [(0, 1), (1, 0)])]
    every = lax.all_gather(value, "head", axis=0)
    return [every[j] for j in range(every.shape[0])]


def local(
    lineup_state,
    pairwise,
    aligned_residue_bounds,
    residue_valid_mask,
    coupling_offset_weight_map,
    triangle_bias_matrix,
    alignment_projection_matrix,
    lineup_readout_weight,
    feedfwd_entry_weight,
    feedfwd_exit_weight,
    pair_projection_matrix,
    pair_output_matrix,
    left_right_maps,
    outer_product_output_matrix,
):
    seqs, length, channels = lineup_state.shape
    rows, _, pair_channels = pairwise.shape
    heads = coupling_offset_weight_map.shape[1]
    pair_heads = triangle_bias_matrix.shape[1]
    every_head = heads + pair_heads
    depth = left_right_maps.shape[2]
    chips = lax.axis_size("rows")
    cores = lax.axis_size("branch")
    parts = lax.axis_size("head")
    width = outer_product_output_matrix.shape[1]
    features = heads * PER_FOCUS_DIM
    pair_features = pair_heads * PER_FOCUS_DIM
    total = chips * cores * seqs
    bounds = aligned_residue_bounds.T

    first = (
        lineup_state,
        pairwise,
        coupling_offset_weight_map.T,
        triangle_bias_matrix.T,
        jnp.swapaxes(left_right_maps, 1, 2),
        bounds,
    )
    (payload,) = call(
        functools.partial(pre_kernel, cores),
        first,
        (((chips, every_head * rows + seqs * depth + rows, length), BF16),),
        scratch=held_copies(first),
        left=range(len(first)),
        grant=60 << 20,
    )
    mine = lax.all_to_all(payload, "rows", 0, 0, tiled=True)
    other = lax.ppermute(mine, "branch", [(0, 1), (1, 0)])

    if parts == 2:
        low, high = feedfwd_exit_weight[:, : channels // 2], feedfwd_exit_weight[:, channels // 2 :]
        own = lax.axis_index("head") == 0
        kept, sent = jnp.where(own, low, high), jnp.where(own, high, low)
        entry = lax.ppermute(feedfwd_entry_weight, "head", [(0, 1), (1, 0)])
        leave = lax.ppermute(sent, "head", [(0, 1), (1, 0)])
        entries, exits = [feedfwd_entry_weight, entry], [kept, leave]
    else:
        entries = lax.all_gather(feedfwd_entry_weight, "head", axis=0)
        exits = lax.all_to_all(feedfwd_exit_weight, "head", 1, 0, tiled=True)
        exits = exits.reshape(parts, -1, exits.shape[1])
        entries, exits = list(entries), list(exits)

    groups = 128 // width
    second = (
        lineup_state,
        pairwise,
        alignment_projection_matrix,
        jnp.swapaxes(pair_projection_matrix, 1, 2),
        outer_product_output_matrix.T,
        bounds,
        residue_valid_mask.reshape(1, -1),
    )
    scores, values, gate, tri_scores, tri_values, tri_gate, own_pair, outer_w, masks, shares = call(
        functools.partial(proj_kernel, cores, heads, pair_heads),
        second,
        (
            ((seqs, heads, length, length), F32),
            ((seqs, length, features), BF16),
            ((seqs, length, features), F32),
            ((rows, pair_heads, length, length), F32),
            ((rows, pair_features, length), BF16),
            ((rows, pair_features, length), F32),
            ((rows, width, length), BF16),
            ((depth, depth * width), BF16),
            ((seqs + 1, length), F32),
            ((rows, length), F32),
        ),
        scratch=[
            *held_copies(second)[:-1],
            pltpu.VMEM((pair_channels, length), F32),
            pltpu.VMEM((depth * depth, 128), F32),
            held_copies(second)[-1],
        ],
        left=range(len(second)),
        flops=1 << 28,
    )

    (mixed,) = call(
        functools.partial(align_kernel, cores, rows),
        (mine, other, scores, values, gate, masks),
        (((seqs, length, features), BF16),),
        scratch=[pltpu.VMEM((heads, length, length), F32)],
        flops=1 << 28,
    )
    mixed = from_heads(mixed)
    (pair_mixed,) = call(
        functools.partial(tri_kernel, cores, heads),
        (mine, other, tri_scores, tri_values, tri_gate, masks),
        (((rows, pair_features, length), BF16),),
        scratch=[pltpu.VMEM((pair_heads, length, length), F32)],
        flops=1 << 28,
    )
    pair_mixed = from_heads(pair_mixed)

    own_width = channels // parts
    (refreshed,) = call(
        functools.partial(transition_kernel, parts),
        (*mixed, lineup_state, lineup_readout_weight, *entries, *exits),
        (((seqs, length, own_width), BF16),),
        scratch=[pltpu.VMEM((channels, seqs * 128), F32)],
        flops=1 << 28,
    )

    (opm,) = call(
        functools.partial(outer_kernel, cores, seqs, every_head),
        (mine, other, outer_w, shares, own_pair),
        (((rows, width, length), F32),),
        scratch=[
            pltpu.VMEM((rows * total, depth * cores * seqs), F32),
            pltpu.VMEM((groups, length // 128, depth // groups * total, 128), F32),
        ],
        flops=1 << 28,
    )
    (pair_out,) = call(
        functools.partial(close_kernel, parts),
        (*pair_mixed, opm, pair_output_matrix.T),
        (((rows, width, length), BF16),),
        flops=1 << 26,
    )
    return (refreshed, jnp.swapaxes(pair_out, 1, 2))


def solution(mesh):
    in_specs = (
        P(("parts", "rows", "branch"), None, None),
        P(("parts", "rows", "branch"), None, None),
        P("parts", None),
        P("parts"),
        P(None, "head"),
        P(None, "head"),
        P(None, None, "head"),
        P(),
        P(None, "head"),
        P("head", None),
        P(None, None, "head"),
        P(None, "head"),
        P(),
        P(None, "head"),
    )
    out_specs = (
        P(("parts", "rows", "branch"), None, "head"),
        P(("parts", "rows", "branch"), None, "head"),
    )


    return jax.shard_map(local, mesh=mesh, in_specs=in_specs, out_specs=out_specs, check_vma=False)
```

```python
import functools
import math

import jax
import jax.numpy as jnp
from jax import lax
from jax.experimental import pallas as pl
from jax.experimental.pallas import tpu as pltpu
from jax.sharding import PartitionSpec as P


PER_FOCUS_DIM = 32
F32 = jnp.float32
BF16 = jnp.bfloat16
LOG2E = math.log2(math.e)
SCALE = LOG2E / math.sqrt(PER_FOCUS_DIM)
FAR = -1.0e30

VMEM = pl.BlockSpec(memory_space=pltpu.VMEM)
HBM = pl.BlockSpec(memory_space=pltpu.HBM)


def nt(a, b):
    return lax.dot_general(a, b, (((1,), (1,)), ((), ())), preferred_element_type=F32)


def nn(a, b):
    return lax.dot_general(a, b, (((1,), (0,)), ((), ())), preferred_element_type=F32)


def normed(values):
    values = values.astype(F32)
    center = values - jnp.mean(values, -1, keepdims=True)
    spread = jnp.mean(center * center, -1, keepdims=True)
    return center * lax.rsqrt(spread + 1e-05)


def places(shape, axis):
    return lax.broadcasted_iota(jnp.int32, shape, axis)


def place_of(cores):
    return lax.axis_index("rows") * cores + lax.axis_index("branch")


def span_of(bounds_ref, which):
    bounds = bounds_ref[...].astype(F32)
    kept = jnp.where(places(bounds.shape, 1) == which, bounds, 0.0)
    span = jnp.sum(kept, axis=1, keepdims=True)
    return span[0:1], span[1:2]


def within(at, begin, end):
    at = at.astype(F32)
    return (at >= begin) & (at < end)


def fetch(pairs, sem):
    copies = [pltpu.make_async_copy(a, b, sem.at[j]) for j, (a, b) in enumerate(pairs)]
    for copy in copies:
        copy.start()
    return copies


def pack_kernel(entry_ref, exit_ref, out_ref, held_ref, sem):
    units = held_ref.shape[0]
    width = held_ref.shape[1] - units
    first = pl.multiple_of(lax.axis_index("branch") * units, units)
    begin = pl.multiple_of((1 - lax.axis_index("head")) * width, width)
    pairs = [
        (entry_ref.at[:, pl.ds(first, units)], held_ref.at[:, pl.ds(0, units)]),
        (exit_ref.at[pl.ds(first, units), pl.ds(begin, width)], held_ref.at[:, pl.ds(units, width)]),
    ]
    for copy in fetch(pairs, sem):
        copy.wait()
    copy = pltpu.make_async_copy(held_ref, out_ref, sem.at[0])
    copy.start()
    copy.wait()


def pre_kernel(cores, *refs):
    pay_ref, held, (bias_ref, factor_ref, in_sem, out_sem) = refs[6], refs[7:13], refs[13:]
    copies = fetch(list(zip(refs[:6], held)), in_sem)
    x_ref, p_ref, mb_ref, tb_ref, lr_ref, bounds_ref = held
    seqs, length, _ = x_ref.shape
    rows = p_ref.shape[0]
    chips = pay_ref.shape[0]
    depth = lr_ref.shape[1]
    first_seq = place_of(cores) * seqs
    for j in (0, 4, 5):
        copies[j].wait()
    pieces = []
    left = None
    zero = jnp.zeros(lr_ref.shape[1:], BF16)
    for s in range(seqs):
        xn = normed(x_ref[s]).astype(BF16)
        begin, end = span_of(bounds_ref, first_seq + s)
        seen = within(places((1, length), 1), begin, end)
        pieces.append(nt(lr_ref[1], xn) * seen.astype(F32))
        weight = jnp.concatenate(
            [lr_ref[0] if other == s else zero for _ in range(cores) for other in range(seqs)],
            axis=0,
        )
        term = nt(xn, weight) * within(places((length, 1), 0), begin, end).astype(F32)
        left = term if left is None else left + term
    right = jnp.concatenate(pieces, axis=0).astype(BF16)
    lanes = left.shape[1]
    group = places((rows, lanes), 1) // (seqs * depth)
    first, count = bias_ref.shape[1], right.shape[0]
    for d in range(chips):
        mine = left[d * cores * rows : d * cores * rows + rows]
        for c in range(1, cores):
            begin = (d * cores + c) * rows
            mine = jnp.where(group == c, left[begin : begin + rows], mine)
        if lanes < length:
            mine = jnp.concatenate([mine, jnp.zeros((rows, length - lanes), F32)], axis=1)
        factor_ref[d, 0:count, :] = right
        factor_ref[d, count : count + rows, :] = mine.astype(BF16)
    sends = [pltpu.make_async_copy(factor_ref, pay_ref.at[:, first:], out_sem.at[0])]
    sends[0].start()
    for j in (1, 2, 3):
        copies[j].wait()
    bias_w = jnp.concatenate([mb_ref[...].astype(F32), tb_ref[...].astype(F32)], axis=0)
    bias_w = bias_w.astype(BF16)
    heads = bias_w.shape[0]
    biases = [nt(bias_w, normed(p_ref[i]).astype(BF16)) for i in range(rows)]
    pieces = [jnp.concatenate([b[h : h + 1] for b in biases], axis=0) for h in range(heads)]
    bias = jnp.concatenate(pieces, axis=0).astype(BF16)
    for d in range(chips):
        bias_ref[d] = bias
    sends.append(pltpu.make_async_copy(bias_ref, pay_ref.at[:, 0:first], out_sem.at[1]))
    sends[1].start()
    for copy in sends:
        copy.wait()


def proj_kernel(cores, heads, pair_heads, *refs):
    count = 7
    sm_ref, v_ref, g_ref, st_ref, pv_ref, pg_ref, own_ref, lay_ref, mask_ref, share_ref = refs[
        count : count + 10
    ]
    held = refs[count + 10 : 2 * count + 10]
    turn_ref, rows_ref, sem = refs[2 * count + 10 :]
    copies = fetch(list(zip(refs[:count], held)), sem)
    x_ref, p_ref, aw_ref, pw_ref, ow_ref, bounds_ref, valid_ref = held
    seqs, length, _ = x_ref.shape
    rows = p_ref.shape[0]
    for copy in copies:
        copy.wait()
    first_seq = place_of(cores) * seqs
    for s in range(seqs):
        begin, end = span_of(bounds_ref, first_seq + s)
        mask_ref[s : s + 1] = jnp.where(within(places((1, length), 1), begin, end), 0.0, FAR)
    mask_ref[seqs : seqs + 1] = jnp.where(valid_ref[...] > 0, 0.0, FAR)
    begin, end = bounds_ref[0:1].astype(F32), bounds_ref[1:2].astype(F32)
    whole = within(places((length, 1), 0), begin, end).astype(BF16)
    owned = within(places((rows, 1), 0) + place_of(cores) * rows, begin, end).astype(BF16)
    share_ref[...] = 1.0 / nt(owned, whole)
    for s in range(seqs):
        xn = normed(x_ref[s]).astype(BF16)
        q = nn(xn, aw_ref[0]).astype(BF16)
        k = nn(xn, aw_ref[1]).astype(BF16)
        v_ref[s] = nn(xn, aw_ref[2]).astype(BF16)
        g_ref[s] = jax.nn.sigmoid(nn(xn, aw_ref[3]))
        head = places(q.shape, 1) // PER_FOCUS_DIM
        for h in range(heads):
            sm_ref[s, h] = nt(jnp.where(head == h, q, jnp.zeros_like(q)), k) * SCALE
    width = own_ref.shape[1]
    begin = pl.multiple_of(lax.axis_index("head") * width, width)
    for i in range(rows):
        pn = normed(p_ref[i]).astype(BF16)
        q = nt(pn, pw_ref[0]).astype(BF16)
        k = nt(pn, pw_ref[1]).astype(BF16)
        pv_ref[i] = nt(pw_ref[2], pn).astype(BF16)
        pg_ref[i] = jax.nn.sigmoid(nt(pw_ref[3], pn))
        head = places(q.shape, 1) // PER_FOCUS_DIM
        for h in range(pair_heads):
            st_ref[i, h] = nt(jnp.where(head == h, q, jnp.zeros_like(q)), k) * SCALE
        turn_ref[...] = p_ref[i].astype(F32).T
        own_ref[i] = turn_ref[pl.ds(begin, width), :].astype(BF16)
    groups = 128 // width
    steps = lay_ref.shape[1] // 128
    depth = steps * groups
    turned = ow_ref[...].astype(F32)
    rows_ref[...] = jnp.concatenate([turned] * groups, axis=0).T
    group = places((depth, 128), 1) // width
    for step in range(steps):
        tile = rows_ref[pl.ds(step, depth, stride=depth), :]
        for g in range(1, groups):
            part = rows_ref[pl.ds(g * steps + step, depth, stride=depth), :]
            tile = jnp.where(group == g, part, tile)
        lay_ref[:, step * 128 : (step + 1) * 128] = tile.astype(BF16)


def gather_bias(bias_ref, mine_ref, other_ref, first, heads, rows, cores):
    chips = mine_ref.shape[0]
    core = lax.axis_index("branch")
    for d in range(chips):
        for ref, c in ((mine_ref, core), (other_ref, 1 - core)):
            begin = pl.multiple_of((d * cores + c) * rows, rows)
            block = ref[d, first * rows : (first + heads) * rows, :].astype(F32) * LOG2E
            for h in range(heads):
                bias_ref[h, pl.ds(begin, rows), :] = block[h * rows : (h + 1) * rows]


def attend(scores, values, gate):
    width = values.shape[1]
    head = places(values.shape, 1) // PER_FOCUS_DIM
    mixed = total = None
    for h, score in enumerate(scores):
        top = jnp.max(score, axis=-1, keepdims=True)
        weights = jnp.exp2(score - top).astype(BF16)
        here = head == h
        value = jnp.where(here, values, jnp.zeros_like(values))
        ones = jnp.where(here, jnp.ones_like(values), jnp.zeros_like(values))
        if width % 128 == 0:
            both = nn(weights, jnp.concatenate([value, ones], axis=1))
            part, norm = both[:, :width], both[:, width:]
        else:
            part, norm = nn(weights, value), nn(weights, ones)
        mixed = part if mixed is None else mixed + part
        total = norm if total is None else total + norm
    return gate * mixed / total


def align_kernel(cores, rows, mine_ref, other_ref, sm_ref, v_ref, g_ref, mask_ref, out_ref, bias_ref):
    seqs, heads, _, _ = sm_ref.shape
    gather_bias(bias_ref, mine_ref, other_ref, 0, heads, rows, cores)
    for s in range(seqs):
        mask = mask_ref[s : s + 1]
        scores = [sm_ref[s, h] + (bias_ref[h] + mask) for h in range(heads)]
        out_ref[s] = attend(scores, v_ref[s], g_ref[s]).astype(BF16)


def tri_kernel(cores, first, mine_ref, other_ref, st_ref, v_ref, g_ref, mask_ref, out_ref, bias_ref):
    rows, heads, length, _ = st_ref.shape
    last = mask_ref.shape[0] - 1
    gather_bias(bias_ref, mine_ref, other_ref, first, heads, rows, cores)
    for h in range(heads):
        bias_ref[h] = bias_ref[h] + mask_ref[last : last + 1]
    ones = jnp.ones((8, length), BF16)
    for i in range(rows):
        for h in range(heads):
            score = st_ref[i, h] + bias_ref[h]
            top = jnp.max(score, axis=-1, keepdims=True)
            weights = jnp.exp2(score - top).astype(BF16)
            at = slice(h * PER_FOCUS_DIM, (h + 1) * PER_FOCUS_DIM)
            mixed = nt(v_ref[i, at, :], weights)
            total = nt(ones, weights)[0:1]
            out_ref[i, at, :] = (g_ref[i, at, :] * mixed / total).astype(BF16)


def transition_kernel(parts, own_only, *refs):
    heads_refs = refs[:parts]
    x_ref, wo_ref = refs[parts : parts + 2]
    count = 1 if own_only else parts
    entry_refs = refs[parts + 2 : parts + 2 + count]
    exit_refs = refs[parts + 2 + count : parts + 2 + 2 * count]
    out_ref, turn_ref = refs[-2:]
    seqs = x_ref.shape[0]
    features = heads_refs[0].shape[2]
    width = out_ref.shape[2]
    here = lax.axis_index("head")

    def owned(value):
        if parts == 2:
            return jnp.where(here == 0, value[:, :width], value[:, width:])
        turn_ref[...] = value.T
        return turn_ref[pl.ds(pl.multiple_of(here * width, width), width), :].T

    if own_only:
        begin = pl.multiple_of(here * width, width)
        weights = [(entry_refs[0][...], exit_refs[0][:, pl.ds(begin, width)])]
        for ref in refs[-4:-2]:
            units = ref.shape[0]
            weights.append((ref[:, :units], ref[:, units:]))
    else:
        weights = [(entry[...], leave[...]) for entry, leave in zip(entry_refs, exit_refs)]
    length = x_ref.shape[1]
    for begin_row in range(0, length, 128):
        at = slice(begin_row, begin_row + 128)
        blended = jnp.concatenate([x_ref[s, at, :] for s in range(seqs)], axis=0).astype(F32)
        for j in range(parts):
            which = jnp.where(j == 0, here, 1 - here) if parts == 2 else j
            begin = pl.multiple_of(which * features, features)
            mixed = jnp.concatenate([heads_refs[j][s, at, :] for s in range(seqs)], axis=0)
            blended = blended + nn(mixed, wo_ref[pl.ds(begin, features), :])
        standardized = normed(blended).astype(BF16)
        out = owned(blended)
        for enter, leave in weights:
            value = jnp.maximum(nn(standardized, enter), 0.0).astype(BF16)
            out = out + nn(value, leave)
        for s in range(seqs):
            out_ref[s, at, :] = out[s * 128 : (s + 1) * 128].astype(BF16)


def outer_kernel(cores, seqs, heads, mine_ref, other_ref, w_ref, share_ref, own_ref, out_ref, a_ref, b_ref):
    rows, width, length = out_ref.shape
    chips = mine_ref.shape[0]
    depth = w_ref.shape[0]
    lanes = depth * cores * seqs
    groups = 128 // width
    steps = depth // groups
    total = chips * cores * seqs
    core = lax.axis_index("branch")
    first = heads * rows
    lane_group = places((rows, lanes), 1) // depth
    for d in range(chips):
        for which, ref in enumerate((mine_ref, other_ref)):
            block = ref[d, first : first + seqs * depth, :].astype(F32)
            left = ref[d, first + seqs * depth : first + seqs * depth + rows, :lanes].astype(F32)
            for s in range(seqs):
                row = (d * cores + which) * seqs + s
                for g in range(groups):
                    begin = s * depth + g * steps
                    for t in range(length // 128):
                        piece = block[begin : begin + steps, t * 128 : (t + 1) * 128]
                        b_ref[g, t, pl.ds(row, steps, stride=total), :] = piece
                kept = jnp.where(lane_group == core * seqs + s, left, 0.0)
                a_ref[pl.ds(row, rows, stride=total), :] = kept
    a = a_ref[...].astype(BF16)
    share = share_ref[...]
    gathered = [[] for _ in range(rows)]
    for step in range(steps):
        tile = jnp.concatenate([w_ref[:, step * 128 : (step + 1) * 128]] * (cores * seqs), axis=0)
        g = nn(a, tile).astype(BF16)
        for i in range(rows):
            gathered[i].append(g[i * total : (i + 1) * total])
    b = [[b_ref[g, t].T.astype(BF16) for t in range(length // 128)] for g in range(groups)]
    for i in range(rows):
        g = jnp.concatenate(gathered[i], axis=0)
        for t in range(length // 128):
            acc = None
            for k in range(groups):
                part = nn(b[k][t], g).T[k * width : (k + 1) * width]
                acc = part if acc is None else acc + part
            at = slice(t * 128, (t + 1) * 128)
            out_ref[i, :, at] = acc * share[i : i + 1, at] + own_ref[i, :, at].astype(F32)


def close_kernel(parts, *refs):
    heads_refs = refs[:parts]
    opm_ref, w_ref, fresh_ref, out_ref, copy_ref, stage_ref, sem = refs[parts:]
    copies = [
        pltpu.make_async_copy(fresh_ref, copy_ref, sem.at[0]),
        pltpu.make_async_copy(stage_ref, out_ref, sem.at[1]),
    ]
    copies[0].start()
    rows = opm_ref.shape[0]
    features = heads_refs[0].shape[1]
    own = lax.axis_index("head") == 0
    weight = w_ref[...]
    if parts == 2:
        first, second = weight[:, :features].astype(F32), weight[:, features:].astype(F32)
        turned = jnp.concatenate([second, first], axis=1)
        weight = jnp.where(own, weight.astype(F32), turned).astype(BF16)
    for i in range(rows):
        every = jnp.concatenate([ref[i] for ref in heads_refs], axis=0)
        stage_ref[i] = (opm_ref[i] + nn(weight, every)).astype(BF16)
    copies[1].start()
    for copy in copies:
        copy.wait()


def call(kernel, ins, outs, scratch=(), left=(), written=(), grant=0, flops=0):
    size = sum(a.size * a.dtype.itemsize for a in ins) + sum(
        math.prod(s) * jnp.dtype(d).itemsize for s, d in outs
    )
    held = sum(a.inner_aval.size * 4 for a in scratch )
    limit = grant or min(max((size + held) * 2, 8 << 20), 60 << 20)
    run = pl.pallas_call(
        kernel,
        compiler_params=pltpu.CompilerParams(vmem_limit_bytes=limit),
        out_shape=tuple(jax.ShapeDtypeStruct(s, d) for s, d in outs),
        in_specs=[HBM if i in left else VMEM for i in range(len(ins))],
        out_specs=tuple(HBM if i in written else VMEM for i in range(len(outs))),
        scratch_shapes=list(scratch),
        cost_estimate=pl.CostEstimate(flops=flops, bytes_accessed=size, transcendentals=0),
    )
    ins = [pltpu.with_memory_space_constraint(a, pltpu.HBM) if i in left else a for i, a in enumerate(ins)]
    return run(*ins)


def held_copies(arrays):
    return [*(pltpu.VMEM(a.shape, a.dtype) for a in arrays), pltpu.SemaphoreType.DMA((len(arrays),))]


def from_heads(value):
    if lax.axis_size("head") == 2:
        return [value, lax.ppermute(value, "head", [(0, 1), (1, 0)])]
    every = lax.all_gather(value, "head", axis=0)
    return [every[j] for j in range(every.shape[0])]


def local(
    lineup_state,
    pairwise,
    aligned_residue_bounds,
    residue_valid_mask,
    coupling_offset_weight_map,
    triangle_bias_matrix,
    alignment_projection_matrix,
    lineup_readout_weight,
    feedfwd_entry_weight,
    feedfwd_exit_weight,
    pair_projection_matrix,
    pair_output_matrix,
    left_right_maps,
    outer_product_output_matrix,
):
    seqs, length, channels = lineup_state.shape
    rows, _, pair_channels = pairwise.shape
    heads = coupling_offset_weight_map.shape[1]
    pair_heads = triangle_bias_matrix.shape[1]
    every_head = heads + pair_heads
    depth = left_right_maps.shape[2]
    chips = lax.axis_size("rows")
    cores = lax.axis_size("branch")
    parts = lax.axis_size("head")
    width = outer_product_output_matrix.shape[1]
    features = heads * PER_FOCUS_DIM
    pair_features = pair_heads * PER_FOCUS_DIM
    total = chips * cores * seqs
    bounds = aligned_residue_bounds.T

    first = (
        lineup_state,
        pairwise,
        coupling_offset_weight_map.T,
        triangle_bias_matrix.T,
        jnp.swapaxes(left_right_maps, 1, 2),
        bounds,
    )
    bias_rows = every_head * rows
    right_rows = seqs * depth
    hidden = feedfwd_entry_weight.shape[1]
    (payload,) = call(
        functools.partial(pre_kernel, cores),
        first,
        (((chips, bias_rows + right_rows + rows, length), BF16),),
        scratch=[
            *held_copies(first)[:-1],
            pltpu.VMEM((chips, bias_rows, length), BF16),
            pltpu.VMEM((chips, right_rows + rows, length), BF16),
            held_copies(first)[-1],
            pltpu.SemaphoreType.DMA((2,)),
        ],
        left=range(len(first)),
        written=(0,),
        grant=60 << 20,
    )
    mine = lax.all_to_all(payload, "rows", 0, 0, tiled=True)
    other = lax.ppermute(mine, "branch", [(0, 1), (1, 0)])

    if parts == 2 and cores == 2 and hidden == cores * channels:
        shape = (channels, hidden // cores + channels // parts)
        (packed,) = call(
            pack_kernel,
            (feedfwd_entry_weight, feedfwd_exit_weight),
            ((shape, BF16),),
            scratch=[pltpu.VMEM(shape, BF16), pltpu.SemaphoreType.DMA((2,))],
            left=(0, 1),
            written=(0,),
            flops=1 << 28,
        )
        others = [lax.ppermute(packed, "head", [(0, 1), (1, 0)])]
        others.append(lax.ppermute(others[0], "branch", [(0, 1), (1, 0)]))
        entries, exits = [feedfwd_entry_weight], [feedfwd_exit_weight]
    else:
        entries = lax.all_gather(feedfwd_entry_weight, "head", axis=0)
        exits = lax.all_to_all(feedfwd_exit_weight, "head", 1, 0, tiled=True)
        exits = exits.reshape(parts, -1, exits.shape[1])
        entries, exits, others = list(entries), list(exits), []

    groups = 128 // width
    second = (
        lineup_state,
        pairwise,
        alignment_projection_matrix,
        jnp.swapaxes(pair_projection_matrix, 1, 2),
        outer_product_output_matrix.T,
        bounds,
        residue_valid_mask.reshape(1, -1),
    )
    scores, values, gate, tri_scores, tri_values, tri_gate, own_pair, outer_w, masks, shares = call(
        functools.partial(proj_kernel, cores, heads, pair_heads),
        second,
        (
            ((seqs, heads, length, length), F32),
            ((seqs, length, features), BF16),
            ((seqs, length, features), F32),
            ((rows, pair_heads, length, length), F32),
            ((rows, pair_features, length), BF16),
            ((rows, pair_features, length), F32),
            ((rows, width, length), BF16),
            ((depth, depth * width), BF16),
            ((seqs + 1, length), F32),
            ((rows, length), F32),
        ),
        scratch=[
            *held_copies(second)[:-1],
            pltpu.VMEM((pair_channels, length), F32),
            pltpu.VMEM((depth * depth, 128), F32),
            held_copies(second)[-1],
        ],
        left=range(len(second)),
        flops=1 << 28,
    )

    (mixed,) = call(
        functools.partial(align_kernel, cores, rows),
        (mine, other, scores, values, gate, masks),
        (((seqs, length, features), BF16),),
        scratch=[pltpu.VMEM((heads, length, length), F32)],
        flops=1 << 28,
    )
    mixed = from_heads(mixed)
    (pair_mixed,) = call(
        functools.partial(tri_kernel, cores, heads),
        (mine, other, tri_scores, tri_values, tri_gate, masks),
        (((rows, pair_features, length), BF16),),
        scratch=[pltpu.VMEM((pair_heads, length, length), F32)],
        flops=1 << 28,
    )
    pair_mixed = from_heads(pair_mixed)

    own_width = channels // parts
    (fresh,) = call(
        functools.partial(transition_kernel, parts, bool(others)),
        (*mixed, lineup_state, lineup_readout_weight, *entries, *exits, *others),
        (((seqs, length, own_width), BF16),),
        scratch=[pltpu.VMEM((channels, seqs * 128), F32)],
        flops=1 << 28,
    )

    (opm,) = call(
        functools.partial(outer_kernel, cores, seqs, every_head),
        (mine, other, outer_w, shares, own_pair),
        (((rows, width, length), F32),),
        scratch=[
            pltpu.VMEM((rows * total, depth * cores * seqs), F32),
            pltpu.VMEM((groups, length // 128, depth // groups * total, 128), F32),
        ],
        flops=1 << 28,
    )
    pair_out, refreshed = call(
        functools.partial(close_kernel, parts),
        (*pair_mixed, opm, pair_output_matrix.T, fresh),
        (((rows, width, length), BF16), (fresh.shape, BF16)),
        scratch=[pltpu.VMEM((rows, width, length), BF16), pltpu.SemaphoreType.DMA((2,))],
        written=(0, 1),
        flops=1 << 26,
    )
    return (refreshed, jnp.swapaxes(pair_out, 1, 2))


def solution(mesh):
    in_specs = (
        P(("parts", "rows", "branch"), None, None),
        P(("parts", "rows", "branch"), None, None),
        P("parts", None),
        P("parts"),
        P(None, "head"),
        P(None, "head"),
        P(None, None, "head"),
        P(),
        P(None, "head"),
        P("head", None),
        P(None, None, "head"),
        P(None, "head"),
        P(),
        P(None, "head"),
    )
    out_specs = (
        P(("parts", "rows", "branch"), None, "head"),
        P(("parts", "rows", "branch"), None, "head"),
    )


    return jax.shard_map(local, mesh=mesh, in_specs=in_specs, out_specs=out_specs, check_vma=False)
```

```python
import functools
import math

import jax
import jax.numpy as jnp
from jax import lax
from jax.experimental import pallas as pl
from jax.experimental.pallas import tpu as pltpu
from jax.sharding import PartitionSpec as P


PER_FOCUS_DIM = 32
F32 = jnp.float32
BF16 = jnp.bfloat16
LOG2E = math.log2(math.e)
SCALE = LOG2E / math.sqrt(PER_FOCUS_DIM)
FAR = -1.0e30

VMEM = pl.BlockSpec(memory_space=pltpu.VMEM)
HBM = pl.BlockSpec(memory_space=pltpu.HBM)


def nt(a, b):
    return lax.dot_general(a, b, (((1,), (1,)), ((), ())), preferred_element_type=F32)


def nn(a, b):
    return lax.dot_general(a, b, (((1,), (0,)), ((), ())), preferred_element_type=F32)


def normed(values):
    values = values.astype(F32)
    center = values - jnp.mean(values, -1, keepdims=True)
    spread = jnp.mean(center * center, -1, keepdims=True)
    return center * lax.rsqrt(spread + 1e-05)


def places(shape, axis):
    return lax.broadcasted_iota(jnp.int32, shape, axis)


def place_of(cores):
    return lax.axis_index("rows") * cores + lax.axis_index("branch")


def span_of(bounds_ref, which):
    bounds = bounds_ref[...].astype(F32)
    kept = jnp.where(places(bounds.shape, 1) == which, bounds, 0.0)
    span = jnp.sum(kept, axis=1, keepdims=True)
    return span[0:1], span[1:2]


def within(at, begin, end):
    at = at.astype(F32)
    return (at >= begin) & (at < end)


def fetch(pairs, sem):
    copies = [pltpu.make_async_copy(a, b, sem.at[j]) for j, (a, b) in enumerate(pairs)]
    for copy in copies:
        copy.start()
    return copies


def pack_kernel(entry_ref, exit_ref, out_ref, held_ref, sem):
    units = held_ref.shape[0]
    width = held_ref.shape[1] - units
    first = pl.multiple_of(lax.axis_index("branch") * units, units)
    begin = pl.multiple_of((1 - lax.axis_index("head")) * width, width)
    pairs = [
        (entry_ref.at[:, pl.ds(first, units)], held_ref.at[:, pl.ds(0, units)]),
        (exit_ref.at[pl.ds(first, units), pl.ds(begin, width)], held_ref.at[:, pl.ds(units, width)]),
    ]
    for copy in fetch(pairs, sem):
        copy.wait()
    copy = pltpu.make_async_copy(held_ref, out_ref, sem.at[0])
    copy.start()
    copy.wait()


def pre_kernel(cores, *refs):
    doubling = len(refs) == 15
    if doubling:
        (near_ref, far_ref), held, in_sem = refs[6:8], refs[8:14], refs[14]
        chips = 8
    else:
        pay_ref, held, (bias_ref, factor_ref, in_sem, out_sem) = refs[6], refs[7:13], refs[13:]
        chips = pay_ref.shape[0]
    copies = fetch(list(zip(refs[:6], held)), in_sem)
    x_ref, p_ref, mb_ref, tb_ref, lr_ref, bounds_ref = held
    seqs, length, _ = x_ref.shape
    rows = p_ref.shape[0]
    depth = lr_ref.shape[1]
    first_seq = place_of(cores) * seqs
    for j in (0, 4, 5):
        copies[j].wait()
    pieces = []
    left = None
    zero = jnp.zeros(lr_ref.shape[1:], BF16)
    for s in range(seqs):
        xn = normed(x_ref[s]).astype(BF16)
        begin, end = span_of(bounds_ref, first_seq + s)
        seen = within(places((1, length), 1), begin, end)
        pieces.append(nt(lr_ref[1], xn) * seen.astype(F32))
        weight = jnp.concatenate(
            [lr_ref[0] if other == s else zero for _ in range(cores) for other in range(seqs)],
            axis=0,
        )
        term = nt(xn, weight) * within(places((length, 1), 0), begin, end).astype(F32)
        left = term if left is None else left + term
    right = jnp.concatenate(pieces, axis=0).astype(BF16)
    lanes = left.shape[1]
    group = places((rows, lanes), 1) // (seqs * depth)
    first, count = (mb_ref.shape[0] + tb_ref.shape[0]) * rows, right.shape[0]
    lefts = []
    for d in range(chips):
        mine = left[d * cores * rows : d * cores * rows + rows]
        for c in range(1, cores):
            begin = (d * cores + c) * rows
            mine = jnp.where(group == c, left[begin : begin + rows], mine)
        if lanes < length:
            mine = jnp.concatenate([mine, jnp.zeros((rows, length - lanes), F32)], axis=1)
        lefts.append(mine)
    if doubling:
        low = lax.axis_index("rows") < chips // 2
        for k, ref in enumerate((near_ref, far_ref)):
            ref[first : first + count, :] = right
            half = chips // 2
            both = [(lefts[j], lefts[half + j])[:: 1 - 2 * k] for j in range(half)]
            chosen = jnp.concatenate([jnp.where(low, x, y) for x, y in both], axis=0)
            ref[first + count : first + count + half * rows, :] = chosen.astype(BF16)
    else:
        for d in range(chips):
            factor_ref[d, 0:count, :] = right
            factor_ref[d, count : count + rows, :] = lefts[d].astype(BF16)
        sends = [pltpu.make_async_copy(factor_ref, pay_ref.at[:, first:], out_sem.at[0])]
        sends[0].start()
    for j in (1, 2, 3):
        copies[j].wait()
    bias_w = jnp.concatenate([mb_ref[...].astype(F32), tb_ref[...].astype(F32)], axis=0)
    bias_w = bias_w.astype(BF16)
    heads = bias_w.shape[0]
    biases = [nt(bias_w, normed(p_ref[i]).astype(BF16)) for i in range(rows)]
    pieces = [jnp.concatenate([b[h : h + 1] for b in biases], axis=0) for h in range(heads)]
    bias = jnp.concatenate(pieces, axis=0).astype(BF16)
    if doubling:
        near_ref[0:first, :] = bias
        far_ref[0:first, :] = bias
        return
    for d in range(chips):
        bias_ref[d] = bias
    sends.append(pltpu.make_async_copy(bias_ref, pay_ref.at[:, 0:first], out_sem.at[1]))
    sends[1].start()
    for copy in sends:
        copy.wait()


def proj_kernel(cores, heads, pair_heads, *refs):
    count = 7
    sm_ref, v_ref, g_ref, st_ref, pv_ref, pg_ref, own_ref, lay_ref, mask_ref, share_ref = refs[
        count : count + 10
    ]
    held = refs[count + 10 : 2 * count + 10]
    turn_ref, rows_ref, sem = refs[2 * count + 10 :]
    copies = fetch(list(zip(refs[:count], held)), sem)
    x_ref, p_ref, aw_ref, pw_ref, ow_ref, bounds_ref, valid_ref = held
    seqs, length, _ = x_ref.shape
    rows = p_ref.shape[0]
    for copy in copies:
        copy.wait()
    first_seq = place_of(cores) * seqs
    for s in range(seqs):
        begin, end = span_of(bounds_ref, first_seq + s)
        mask_ref[s : s + 1] = jnp.where(within(places((1, length), 1), begin, end), 0.0, FAR)
    mask_ref[seqs : seqs + 1] = jnp.where(valid_ref[...] > 0, 0.0, FAR)
    begin, end = bounds_ref[0:1].astype(F32), bounds_ref[1:2].astype(F32)
    whole = within(places((length, 1), 0), begin, end).astype(BF16)
    owned = within(places((rows, 1), 0) + place_of(cores) * rows, begin, end).astype(BF16)
    share_ref[...] = 1.0 / nt(owned, whole)
    for s in range(seqs):
        xn = normed(x_ref[s]).astype(BF16)
        q = nn(xn, aw_ref[0]).astype(BF16)
        k = nn(xn, aw_ref[1]).astype(BF16)
        v_ref[s] = nn(xn, aw_ref[2]).astype(BF16)
        g_ref[s] = jax.nn.sigmoid(nn(xn, aw_ref[3]))
        head = places(q.shape, 1) // PER_FOCUS_DIM
        for h in range(heads):
            sm_ref[s, h] = nt(jnp.where(head == h, q, jnp.zeros_like(q)), k) * SCALE
    width = own_ref.shape[1]
    begin = pl.multiple_of(lax.axis_index("head") * width, width)
    for i in range(rows):
        pn = normed(p_ref[i]).astype(BF16)
        q = nt(pn, pw_ref[0]).astype(BF16)
        k = nt(pn, pw_ref[1]).astype(BF16)
        pv_ref[i] = nt(pw_ref[2], pn).astype(BF16)
        pg_ref[i] = jax.nn.sigmoid(nt(pw_ref[3], pn))
        head = places(q.shape, 1) // PER_FOCUS_DIM
        for h in range(pair_heads):
            st_ref[i, h] = nt(jnp.where(head == h, q, jnp.zeros_like(q)), k) * SCALE
        turn_ref[...] = p_ref[i].astype(F32).T
        own_ref[i] = turn_ref[pl.ds(begin, width), :].astype(BF16)
    groups = 128 // width
    steps = lay_ref.shape[1] // 128
    depth = steps * groups
    turned = ow_ref[...].astype(F32)
    rows_ref[...] = jnp.concatenate([turned] * groups, axis=0).T
    group = places((depth, 128), 1) // width
    for step in range(steps):
        tile = rows_ref[pl.ds(step, depth, stride=depth), :]
        for g in range(1, groups):
            part = rows_ref[pl.ds(g * steps + step, depth, stride=depth), :]
            tile = jnp.where(group == g, part, tile)
        lay_ref[:, step * 128 : (step + 1) * 128] = tile.astype(BF16)


def sources(refs):
    core = lax.axis_index("branch")
    half = len(refs) // 2
    pairs = list(zip(refs[:half], refs[half:]))
    found = []
    if half == 1:
        for d in range(refs[0].shape[0]):
            for ref, c in zip(pairs[0], (core, 1 - core)):
                found.append((lambda lo, hi, ref=ref, d=d: ref[d, lo:hi, :], d, c))
        return found
    chip = lax.axis_index("rows")
    for e, pair in enumerate(pairs):
        count = pair[0].shape[0] // 2
        for k in range(2):
            for ref, c in zip(pair, (core, 1 - core)):
                read = lambda lo, hi, ref=ref, at=k * count: ref[at + lo : at + hi, :]
                found.append((read, chip ^ (e + 4 * k), c))
    return found


def gather_bias(bias_ref, refs, first, heads, rows, cores):
    for read, d, c in sources(refs):
        begin = pl.multiple_of((d * cores + c) * rows, rows)
        block = read(first * rows, (first + heads) * rows).astype(F32) * LOG2E
        for h in range(heads):
            bias_ref[h, pl.ds(begin, rows), :] = block[h * rows : (h + 1) * rows]


def attend(scores, values, gate):
    width = values.shape[1]
    head = places(values.shape, 1) // PER_FOCUS_DIM
    mixed = total = None
    for h, score in enumerate(scores):
        top = jnp.max(score, axis=-1, keepdims=True)
        weights = jnp.exp2(score - top).astype(BF16)
        here = head == h
        value = jnp.where(here, values, jnp.zeros_like(values))
        ones = jnp.where(here, jnp.ones_like(values), jnp.zeros_like(values))
        if width % 128 == 0:
            both = nn(weights, jnp.concatenate([value, ones], axis=1))
            part, norm = both[:, :width], both[:, width:]
        else:
            part, norm = nn(weights, value), nn(weights, ones)
        mixed = part if mixed is None else mixed + part
        total = norm if total is None else total + norm
    return gate * mixed / total


def align_kernel(cores, rows, *refs):
    gathered, (sm_ref, v_ref, g_ref, mask_ref, out_ref, bias_ref) = refs[:-6], refs[-6:]
    seqs, heads, _, _ = sm_ref.shape
    gather_bias(bias_ref, gathered, 0, heads, rows, cores)
    for s in range(seqs):
        mask = mask_ref[s : s + 1]
        scores = [sm_ref[s, h] + (bias_ref[h] + mask) for h in range(heads)]
        out_ref[s] = attend(scores, v_ref[s], g_ref[s]).astype(BF16)


def tri_kernel(cores, first, *refs):
    gathered, (st_ref, v_ref, g_ref, mask_ref, out_ref, bias_ref) = refs[:-6], refs[-6:]
    rows, heads, length, _ = st_ref.shape
    last = mask_ref.shape[0] - 1
    gather_bias(bias_ref, gathered, first, heads, rows, cores)
    for h in range(heads):
        bias_ref[h] = bias_ref[h] + mask_ref[last : last + 1]
    ones = jnp.ones((8, length), BF16)
    for i in range(rows):
        for h in range(heads):
            score = st_ref[i, h] + bias_ref[h]
            top = jnp.max(score, axis=-1, keepdims=True)
            weights = jnp.exp2(score - top).astype(BF16)
            at = slice(h * PER_FOCUS_DIM, (h + 1) * PER_FOCUS_DIM)
            mixed = nt(v_ref[i, at, :], weights)
            total = nt(ones, weights)[0:1]
            out_ref[i, at, :] = (g_ref[i, at, :] * mixed / total).astype(BF16)


def transition_kernel(parts, own_only, *refs):
    heads_refs = refs[:parts]
    x_ref, wo_ref = refs[parts : parts + 2]
    count = 1 if own_only else parts
    entry_refs = refs[parts + 2 : parts + 2 + count]
    exit_refs = refs[parts + 2 + count : parts + 2 + 2 * count]
    out_ref, turn_ref = refs[-2:]
    seqs = x_ref.shape[0]
    features = heads_refs[0].shape[2]
    width = out_ref.shape[2]
    here = lax.axis_index("head")

    def owned(value):
        if parts == 2:
            return jnp.where(here == 0, value[:, :width], value[:, width:])
        turn_ref[...] = value.T
        return turn_ref[pl.ds(pl.multiple_of(here * width, width), width), :].T

    if own_only:
        begin = pl.multiple_of(here * width, width)
        weights = [(entry_refs[0][...], exit_refs[0][:, pl.ds(begin, width)])]
        for ref in refs[-4:-2]:
            units = ref.shape[0]
            weights.append((ref[:, :units], ref[:, units:]))
    else:
        weights = [(entry[...], leave[...]) for entry, leave in zip(entry_refs, exit_refs)]
    length = x_ref.shape[1]
    for begin_row in range(0, length, 128):
        at = slice(begin_row, begin_row + 128)
        blended = jnp.concatenate([x_ref[s, at, :] for s in range(seqs)], axis=0).astype(F32)
        for j in range(parts):
            which = jnp.where(j == 0, here, 1 - here) if parts == 2 else j
            begin = pl.multiple_of(which * features, features)
            mixed = jnp.concatenate([heads_refs[j][s, at, :] for s in range(seqs)], axis=0)
            blended = blended + nn(mixed, wo_ref[pl.ds(begin, features), :])
        standardized = normed(blended).astype(BF16)
        out = owned(blended)
        for enter, leave in weights:
            value = jnp.maximum(nn(standardized, enter), 0.0).astype(BF16)
            out = out + nn(value, leave)
        for s in range(seqs):
            out_ref[s, at, :] = out[s * 128 : (s + 1) * 128].astype(BF16)


def outer_kernel(cores, seqs, heads, *refs):
    found, (w_ref, share_ref, own_ref, out_ref, a_ref, b_ref) = sources(refs[:-6]), refs[-6:]
    doubling = len(refs) > 8
    rows, width, length = out_ref.shape
    depth = w_ref.shape[0]
    lanes = depth * cores * seqs
    groups = 128 // width
    steps = depth // groups
    total = len(found) * seqs
    core = lax.axis_index("branch")
    first = heads * rows
    last = first + seqs * depth
    lane_group = places((rows, lanes), 1) // depth
    slot = lax.axis_index("rows") % 4
    for at_source, (read, _, _) in enumerate(found):
        block = read(first, last).astype(F32)
        left = read(last, last + rows)[:, :lanes].astype(F32)
        if doubling:
            every = read(last, last + 4 * rows)[:, :lanes].astype(F32)
            for k in range(1, 4):
                left = jnp.where(slot == k, every[k * rows : (k + 1) * rows], left)
        for s in range(seqs):
            row = at_source * seqs + s
            for g in range(groups):
                begin = s * depth + g * steps
                for t in range(length // 128):
                    piece = block[begin : begin + steps, t * 128 : (t + 1) * 128]
                    b_ref[g, t, pl.ds(row, steps, stride=total), :] = piece
            kept = jnp.where(lane_group == core * seqs + s, left, 0.0)
            a_ref[pl.ds(row, rows, stride=total), :] = kept
    a = a_ref[...].astype(BF16)
    share = share_ref[...]
    gathered = [[] for _ in range(rows)]
    for step in range(steps):
        tile = jnp.concatenate([w_ref[:, step * 128 : (step + 1) * 128]] * (cores * seqs), axis=0)
        g = nn(a, tile).astype(BF16)
        for i in range(rows):
            gathered[i].append(g[i * total : (i + 1) * total])
    b = [[b_ref[g, t].T.astype(BF16) for t in range(length // 128)] for g in range(groups)]
    for i in range(rows):
        g = jnp.concatenate(gathered[i], axis=0)
        for t in range(length // 128):
            acc = None
            for k in range(groups):
                part = nn(b[k][t], g).T[k * width : (k + 1) * width]
                acc = part if acc is None else acc + part
            at = slice(t * 128, (t + 1) * 128)
            out_ref[i, :, at] = acc * share[i : i + 1, at] + own_ref[i, :, at].astype(F32)


def close_kernel(parts, *refs):
    heads_refs = refs[:parts]
    opm_ref, w_ref, fresh_ref, out_ref, copy_ref, stage_ref, sem = refs[parts:]
    copies = [
        pltpu.make_async_copy(fresh_ref, copy_ref, sem.at[0]),
        pltpu.make_async_copy(stage_ref, out_ref, sem.at[1]),
    ]
    copies[0].start()
    rows = opm_ref.shape[0]
    features = heads_refs[0].shape[1]
    own = lax.axis_index("head") == 0
    weight = w_ref[...]
    if parts == 2:
        first, second = weight[:, :features].astype(F32), weight[:, features:].astype(F32)
        turned = jnp.concatenate([second, first], axis=1)
        weight = jnp.where(own, weight.astype(F32), turned).astype(BF16)
    for i in range(rows):
        every = jnp.concatenate([ref[i] for ref in heads_refs], axis=0)
        stage_ref[i] = (opm_ref[i] + nn(weight, every)).astype(BF16)
    copies[1].start()
    for copy in copies:
        copy.wait()


def call(kernel, ins, outs, scratch=(), left=(), written=(), grant=0, flops=0):
    size = sum(a.size * a.dtype.itemsize for a in ins) + sum(
        math.prod(s) * jnp.dtype(d).itemsize for s, d in outs
    )
    held = sum(a.inner_aval.size * 4 for a in scratch )
    limit = grant or min(max((size + held) * 2, 8 << 20), 60 << 20)
    run = pl.pallas_call(
        kernel,
        compiler_params=pltpu.CompilerParams(vmem_limit_bytes=limit),
        out_shape=tuple(jax.ShapeDtypeStruct(s, d) for s, d in outs),
        in_specs=[HBM if i in left else VMEM for i in range(len(ins))],
        out_specs=tuple(HBM if i in written else VMEM for i in range(len(outs))),
        scratch_shapes=list(scratch),
        cost_estimate=pl.CostEstimate(flops=flops, bytes_accessed=size, transcendentals=0),
    )
    ins = [pltpu.with_memory_space_constraint(a, pltpu.HBM) if i in left else a for i, a in enumerate(ins)]
    return run(*ins)


def held_copies(arrays):
    return [*(pltpu.VMEM(a.shape, a.dtype) for a in arrays), pltpu.SemaphoreType.DMA((len(arrays),))]


def from_heads(value):
    if lax.axis_size("head") == 2:
        return [value, lax.ppermute(value, "head", [(0, 1), (1, 0)])]
    every = lax.all_gather(value, "head", axis=0)
    return [every[j] for j in range(every.shape[0])]


def local(
    lineup_state,
    pairwise,
    aligned_residue_bounds,
    residue_valid_mask,
    coupling_offset_weight_map,
    triangle_bias_matrix,
    alignment_projection_matrix,
    lineup_readout_weight,
    feedfwd_entry_weight,
    feedfwd_exit_weight,
    pair_projection_matrix,
    pair_output_matrix,
    left_right_maps,
    outer_product_output_matrix,
):
    seqs, length, channels = lineup_state.shape
    rows, _, pair_channels = pairwise.shape
    heads = coupling_offset_weight_map.shape[1]
    pair_heads = triangle_bias_matrix.shape[1]
    every_head = heads + pair_heads
    depth = left_right_maps.shape[2]
    chips = lax.axis_size("rows")
    cores = lax.axis_size("branch")
    parts = lax.axis_size("head")
    width = outer_product_output_matrix.shape[1]
    features = heads * PER_FOCUS_DIM
    pair_features = pair_heads * PER_FOCUS_DIM
    total = chips * cores * seqs
    bounds = aligned_residue_bounds.T

    first = (
        lineup_state,
        pairwise,
        coupling_offset_weight_map.T,
        triangle_bias_matrix.T,
        jnp.swapaxes(left_right_maps, 1, 2),
        bounds,
    )
    bias_rows = every_head * rows
    right_rows = seqs * depth
    hidden = feedfwd_entry_weight.shape[1]
    swap = [(0, 1), (1, 0)]
    if chips == 8 and cores == 2:
        shape = (bias_rows + right_rows + chips // 2 * rows, length)
        near, far = call(
            functools.partial(pre_kernel, cores),
            first,
            ((shape, BF16), (shape, BF16)),
            scratch=held_copies(first),
            left=range(len(first)),
        )
        far = lax.ppermute(far, "rows", [(i, i ^ 4) for i in range(8)])
        both = jnp.concatenate([near, far], axis=0)
        mine = [both]
        for e in range(1, 4):
            mine.append(lax.ppermute(both, "rows", [(i, i ^ e) for i in range(8)]))
        other = []
        for e in range(4):
            other.append(lax.ppermute(mine[e], "branch", swap))
    else:
        (payload,) = call(
            functools.partial(pre_kernel, cores),
            first,
            (((chips, bias_rows + right_rows + rows, length), BF16),),
            scratch=[
                *held_copies(first)[:-1],
                pltpu.VMEM((chips, bias_rows, length), BF16),
                pltpu.VMEM((chips, right_rows + rows, length), BF16),
                held_copies(first)[-1],
                pltpu.SemaphoreType.DMA((2,)),
            ],
            left=range(len(first)),
            written=(0,),
            grant=60 << 20,
        )
        mine = [lax.all_to_all(payload, "rows", 0, 0, tiled=True)]
        other = [lax.ppermute(mine[0], "branch", swap)]

    if parts == 2 and cores == 2 and hidden == cores * channels:
        shape = (channels, hidden // cores + channels // parts)
        (packed,) = call(
            pack_kernel,
            (feedfwd_entry_weight, feedfwd_exit_weight),
            ((shape, BF16),),
            scratch=[pltpu.VMEM(shape, BF16), pltpu.SemaphoreType.DMA((2,))],
            left=(0, 1),
            written=(0,),
            flops=1 << 28,
        )
        others = [lax.ppermute(packed, "head", [(0, 1), (1, 0)])]
        others.append(lax.ppermute(others[0], "branch", [(0, 1), (1, 0)]))
        entries, exits = [feedfwd_entry_weight], [feedfwd_exit_weight]
    else:
        entries = lax.all_gather(feedfwd_entry_weight, "head", axis=0)
        exits = lax.all_to_all(feedfwd_exit_weight, "head", 1, 0, tiled=True)
        exits = exits.reshape(parts, -1, exits.shape[1])
        entries, exits, others = list(entries), list(exits), []

    groups = 128 // width
    second = (
        lineup_state,
        pairwise,
        alignment_projection_matrix,
        jnp.swapaxes(pair_projection_matrix, 1, 2),
        outer_product_output_matrix.T,
        bounds,
        residue_valid_mask.reshape(1, -1),
    )
    scores, values, gate, tri_scores, tri_values, tri_gate, own_pair, outer_w, masks, shares = call(
        functools.partial(proj_kernel, cores, heads, pair_heads),
        second,
        (
            ((seqs, heads, length, length), F32),
            ((seqs, length, features), BF16),
            ((seqs, length, features), F32),
            ((rows, pair_heads, length, length), F32),
            ((rows, pair_features, length), BF16),
            ((rows, pair_features, length), F32),
            ((rows, width, length), BF16),
            ((depth, depth * width), BF16),
            ((seqs + 1, length), F32),
            ((rows, length), F32),
        ),
        scratch=[
            *held_copies(second)[:-1],
            pltpu.VMEM((pair_channels, length), F32),
            pltpu.VMEM((depth * depth, 128), F32),
            held_copies(second)[-1],
        ],
        left=range(len(second)),
        flops=1 << 28,
    )

    (mixed,) = call(
        functools.partial(align_kernel, cores, rows),
        (*mine, *other, scores, values, gate, masks),
        (((seqs, length, features), BF16),),
        scratch=[pltpu.VMEM((heads, length, length), F32)],
        flops=1 << 28,
    )
    mixed = from_heads(mixed)
    (pair_mixed,) = call(
        functools.partial(tri_kernel, cores, heads),
        (*mine, *other, tri_scores, tri_values, tri_gate, masks),
        (((rows, pair_features, length), BF16),),
        scratch=[pltpu.VMEM((pair_heads, length, length), F32)],
        flops=1 << 28,
    )
    pair_mixed = from_heads(pair_mixed)

    own_width = channels // parts
    (fresh,) = call(
        functools.partial(transition_kernel, parts, bool(others)),
        (*mixed, lineup_state, lineup_readout_weight, *entries, *exits, *others),
        (((seqs, length, own_width), BF16),),
        scratch=[pltpu.VMEM((channels, seqs * 128), F32)],
        flops=1 << 28,
    )

    (opm,) = call(
        functools.partial(outer_kernel, cores, seqs, every_head),
        (*mine, *other, outer_w, shares, own_pair),
        (((rows, width, length), F32),),
        scratch=[
            pltpu.VMEM((rows * total, depth * cores * seqs), F32),
            pltpu.VMEM((groups, length // 128, depth // groups * total, 128), F32),
        ],
        flops=1 << 28,
    )
    pair_out, refreshed = call(
        functools.partial(close_kernel, parts),
        (*pair_mixed, opm, pair_output_matrix.T, fresh),
        (((rows, width, length), BF16), (fresh.shape, BF16)),
        scratch=[pltpu.VMEM((rows, width, length), BF16), pltpu.SemaphoreType.DMA((2,))],
        written=(0, 1),
        flops=1 << 26,
    )
    return (refreshed, jnp.swapaxes(pair_out, 1, 2))


def solution(mesh):
    in_specs = (
        P(("parts", "rows", "branch"), None, None),
        P(("parts", "rows", "branch"), None, None),
        P("parts", None),
        P("parts"),
        P(None, "head"),
        P(None, "head"),
        P(None, None, "head"),
        P(),
        P(None, "head"),
        P("head", None),
        P(None, None, "head"),
        P(None, "head"),
        P(),
        P(None, "head"),
    )
    out_specs = (
        P(("parts", "rows", "branch"), None, "head"),
        P(("parts", "rows", "branch"), None, "head"),
    )


    return jax.shard_map(local, mesh=mesh, in_specs=in_specs, out_specs=out_specs, check_vma=False)
```

```python
import functools
import math

import jax
import jax.numpy as jnp
from jax import lax
from jax.experimental import pallas as pl
from jax.experimental.pallas import tpu as pltpu
from jax.sharding import PartitionSpec as P


PER_FOCUS_DIM = 32
F32 = jnp.float32
BF16 = jnp.bfloat16
LOG2E = math.log2(math.e)
SCALE = LOG2E / math.sqrt(PER_FOCUS_DIM)
FAR = -1.0e30

VMEM = pl.BlockSpec(memory_space=pltpu.VMEM)
HBM = pl.BlockSpec(memory_space=pltpu.HBM)


def nt(a, b):
    return lax.dot_general(a, b, (((1,), (1,)), ((), ())), preferred_element_type=F32)


def nn(a, b):
    return lax.dot_general(a, b, (((1,), (0,)), ((), ())), preferred_element_type=F32)


def normed(values):
    values = values.astype(F32)
    center = values - jnp.mean(values, -1, keepdims=True)
    spread = jnp.mean(center * center, -1, keepdims=True)
    return center * lax.rsqrt(spread + 1e-05)


def places(shape, axis):
    return lax.broadcasted_iota(jnp.int32, shape, axis)


def place_of(cores):
    return lax.axis_index("rows") * cores + lax.axis_index("branch")


def span_of(bounds_ref, which):
    bounds = bounds_ref[...].astype(F32)
    kept = jnp.where(places(bounds.shape, 1) == which, bounds, 0.0)
    span = jnp.sum(kept, axis=1, keepdims=True)
    return span[0:1], span[1:2]


def within(at, begin, end):
    at = at.astype(F32)
    return (at >= begin) & (at < end)


def fetch(pairs, sem):
    copies = [pltpu.make_async_copy(a, b, sem.at[j]) for j, (a, b) in enumerate(pairs)]
    for copy in copies:
        copy.start()
    return copies


def pack_copies(entry_ref, exit_ref, held_ref):
    units = held_ref.shape[0]
    width = held_ref.shape[1] - units
    first = pl.multiple_of(lax.axis_index("branch") * units, units)
    begin = pl.multiple_of((1 - lax.axis_index("head")) * width, width)
    return [
        (entry_ref.at[:, pl.ds(first, units)], held_ref.at[:, pl.ds(0, units)]),
        (exit_ref.at[pl.ds(first, units), pl.ds(begin, width)], held_ref.at[:, pl.ds(units, width)]),
    ]


def pack_kernel(entry_ref, exit_ref, out_ref, sem):
    for copy in fetch(pack_copies(entry_ref, exit_ref, out_ref), sem):
        copy.wait()


def pre_kernel(cores, doubling, *refs):
    packs = []
    if len(refs) > 15 and doubling:
        entry_ref, exit_ref, packed_ref, pack_sem = refs[6], refs[7], refs[10], refs[-1]
        refs = refs[:6] + refs[8:10] + refs[11:-1]
        packs = pack_copies(entry_ref, exit_ref, packed_ref)
    if doubling:
        (near_ref, far_ref), held, in_sem = refs[6:8], refs[8:14], refs[14]
        chips = 8
    else:
        pay_ref, held, (bias_ref, factor_ref, in_sem, out_sem) = refs[6], refs[7:13], refs[13:]
        chips = pay_ref.shape[0]
    copies = fetch(list(zip(refs[:6], held)), in_sem)
    if packs:
        packs = fetch(packs, pack_sem)
    x_ref, p_ref, mb_ref, tb_ref, lr_ref, bounds_ref = held
    seqs, length, _ = x_ref.shape
    rows = p_ref.shape[0]
    depth = lr_ref.shape[1]
    first_seq = place_of(cores) * seqs
    for j in (0, 4, 5):
        copies[j].wait()
    pieces = []
    left = None
    zero = jnp.zeros(lr_ref.shape[1:], BF16)
    for s in range(seqs):
        xn = normed(x_ref[s]).astype(BF16)
        begin, end = span_of(bounds_ref, first_seq + s)
        seen = within(places((1, length), 1), begin, end)
        pieces.append(nt(lr_ref[1], xn) * seen.astype(F32))
        weight = jnp.concatenate(
            [lr_ref[0] if other == s else zero for _ in range(cores) for other in range(seqs)],
            axis=0,
        )
        term = nt(xn, weight) * within(places((length, 1), 0), begin, end).astype(F32)
        left = term if left is None else left + term
    right = jnp.concatenate(pieces, axis=0).astype(BF16)
    lanes = left.shape[1]
    group = places((rows, lanes), 1) // (seqs * depth)
    first, count = (mb_ref.shape[0] + tb_ref.shape[0]) * rows, right.shape[0]
    lefts = []
    for d in range(chips):
        mine = left[d * cores * rows : d * cores * rows + rows]
        for c in range(1, cores):
            begin = (d * cores + c) * rows
            mine = jnp.where(group == c, left[begin : begin + rows], mine)
        if lanes < length:
            mine = jnp.concatenate([mine, jnp.zeros((rows, length - lanes), F32)], axis=1)
        lefts.append(mine)
    if doubling:
        low = lax.axis_index("rows") < chips // 2
        for k, ref in enumerate((near_ref, far_ref)):
            ref[first : first + count, :] = right
            half = chips // 2
            both = [(lefts[j], lefts[half + j])[:: 1 - 2 * k] for j in range(half)]
            chosen = jnp.concatenate([jnp.where(low, x, y) for x, y in both], axis=0)
            ref[first + count : first + count + half * rows, :] = chosen.astype(BF16)
    else:
        for d in range(chips):
            factor_ref[d, 0:count, :] = right
            factor_ref[d, count : count + rows, :] = lefts[d].astype(BF16)
        sends = [pltpu.make_async_copy(factor_ref, pay_ref.at[:, first:], out_sem.at[0])]
        sends[0].start()
    for j in (1, 2, 3):
        copies[j].wait()
    bias_w = jnp.concatenate([mb_ref[...].astype(F32), tb_ref[...].astype(F32)], axis=0)
    bias_w = bias_w.astype(BF16)
    heads = bias_w.shape[0]
    biases = [nt(bias_w, normed(p_ref[i]).astype(BF16)) for i in range(rows)]
    pieces = [jnp.concatenate([b[h : h + 1] for b in biases], axis=0) for h in range(heads)]
    bias = jnp.concatenate(pieces, axis=0).astype(BF16)
    if doubling:
        near_ref[0:first, :] = bias
        far_ref[0:first, :] = bias
        for copy in packs:
            copy.wait()
        return
    for d in range(chips):
        bias_ref[d] = bias
    sends.append(pltpu.make_async_copy(bias_ref, pay_ref.at[:, 0:first], out_sem.at[1]))
    sends[1].start()
    for copy in sends:
        copy.wait()


def msa_kernel(cores, heads, rows, *refs):
    sm_ref, v_ref, g_ref, mask_ref, share_ref = refs[4:9]
    held, sem = refs[9:13], refs[13]
    copies = fetch(list(zip(refs[:4], held)), sem)
    x_ref, aw_ref, bounds_ref, valid_ref = held
    seqs, length, _ = x_ref.shape
    for copy in copies:
        copy.wait()
    first_seq = place_of(cores) * seqs
    for s in range(seqs):
        begin, end = span_of(bounds_ref, first_seq + s)
        mask_ref[s : s + 1] = jnp.where(within(places((1, length), 1), begin, end), 0.0, FAR)
    mask_ref[seqs : seqs + 1] = jnp.where(valid_ref[...] > 0, 0.0, FAR)
    begin, end = bounds_ref[0:1].astype(F32), bounds_ref[1:2].astype(F32)
    whole = within(places((length, 1), 0), begin, end).astype(BF16)
    owned = within(places((rows, 1), 0) + place_of(cores) * rows, begin, end).astype(BF16)
    share_ref[...] = 1.0 / nt(owned, whole)
    for s in range(seqs):
        xn = normed(x_ref[s]).astype(BF16)
        q = nn(xn, aw_ref[0]).astype(BF16)
        k = nn(xn, aw_ref[1]).astype(BF16)
        v_ref[s] = nn(xn, aw_ref[2]).astype(BF16)
        g_ref[s] = jax.nn.sigmoid(nn(xn, aw_ref[3]))
        head = places(q.shape, 1) // PER_FOCUS_DIM
        for h in range(heads):
            sm_ref[s, h] = nt(jnp.where(head == h, q, jnp.zeros_like(q)), k) * SCALE


def pair_kernel(pair_heads, p_ref, pw_ref, ow_ref, st_ref, pv_ref, pg_ref, own_ref, lay_ref, turn_ref, rows_ref):
    rows = p_ref.shape[0]
    width = own_ref.shape[1]
    begin = pl.multiple_of(lax.axis_index("head") * width, width)
    for i in range(rows):
        pn = normed(p_ref[i]).astype(BF16)
        q = nt(pn, pw_ref[0]).astype(BF16)
        k = nt(pn, pw_ref[1]).astype(BF16)
        pv_ref[i] = nt(pw_ref[2], pn).astype(BF16)
        pg_ref[i] = jax.nn.sigmoid(nt(pw_ref[3], pn))
        head = places(q.shape, 1) // PER_FOCUS_DIM
        for h in range(pair_heads):
            st_ref[i, h] = nt(jnp.where(head == h, q, jnp.zeros_like(q)), k) * SCALE
        turn_ref[...] = p_ref[i].astype(F32).T
        own_ref[i] = turn_ref[pl.ds(begin, width), :].astype(BF16)
    groups = 128 // width
    steps = lay_ref.shape[1] // 128
    depth = steps * groups
    turned = ow_ref[...].astype(F32)
    rows_ref[...] = jnp.concatenate([turned] * groups, axis=0).T
    group = places((depth, 128), 1) // width
    for step in range(steps):
        tile = rows_ref[pl.ds(step, depth, stride=depth), :]
        for g in range(1, groups):
            part = rows_ref[pl.ds(g * steps + step, depth, stride=depth), :]
            tile = jnp.where(group == g, part, tile)
        lay_ref[:, step * 128 : (step + 1) * 128] = tile.astype(BF16)


def sources(refs):
    core = lax.axis_index("branch")
    half = len(refs) // 2
    pairs = list(zip(refs[:half], refs[half:]))
    found = []
    if half == 1:
        for d in range(refs[0].shape[0]):
            for ref, c in zip(pairs[0], (core, 1 - core)):
                found.append((lambda lo, hi, ref=ref, d=d: ref[d, lo:hi, :], d, c))
        return found
    chip = lax.axis_index("rows")
    for e, pair in enumerate(pairs):
        count = pair[0].shape[0] // 2
        for k in range(2):
            for ref, c in zip(pair, (core, 1 - core)):
                read = lambda lo, hi, ref=ref, at=k * count: ref[at + lo : at + hi, :]
                found.append((read, chip ^ (e + 4 * k), c))
    return found


def gather_bias(bias_ref, refs, first, heads, rows, cores):
    for read, d, c in sources(refs):
        begin = pl.multiple_of((d * cores + c) * rows, rows)
        block = read(first * rows, (first + heads) * rows).astype(F32) * LOG2E
        for h in range(heads):
            bias_ref[h, pl.ds(begin, rows), :] = block[h * rows : (h + 1) * rows]


def attend(scores, values, gate):
    width = values.shape[1]
    head = places(values.shape, 1) // PER_FOCUS_DIM
    mixed = total = None
    for h, score in enumerate(scores):
        top = jnp.max(score, axis=-1, keepdims=True)
        weights = jnp.exp2(score - top).astype(BF16)
        here = head == h
        value = jnp.where(here, values, jnp.zeros_like(values))
        ones = jnp.where(here, jnp.ones_like(values), jnp.zeros_like(values))
        if width % 128 == 0:
            both = nn(weights, jnp.concatenate([value, ones], axis=1))
            part, norm = both[:, :width], both[:, width:]
        else:
            part, norm = nn(weights, value), nn(weights, ones)
        mixed = part if mixed is None else mixed + part
        total = norm if total is None else total + norm
    return gate * mixed / total


def align_kernel(cores, rows, *refs):
    gathered, (sm_ref, v_ref, g_ref, mask_ref, out_ref, bias_ref) = refs[:-6], refs[-6:]
    seqs, heads, _, _ = sm_ref.shape
    gather_bias(bias_ref, gathered, 0, heads, rows, cores)
    for s in range(seqs):
        mask = mask_ref[s : s + 1]
        scores = [sm_ref[s, h] + (bias_ref[h] + mask) for h in range(heads)]
        out_ref[s] = attend(scores, v_ref[s], g_ref[s]).astype(BF16)


def tri_kernel(cores, first, *refs):
    gathered, (st_ref, v_ref, g_ref, mask_ref, out_ref, bias_ref) = refs[:-6], refs[-6:]
    rows, heads, length, _ = st_ref.shape
    last = mask_ref.shape[0] - 1
    gather_bias(bias_ref, gathered, first, heads, rows, cores)
    for h in range(heads):
        bias_ref[h] = bias_ref[h] + mask_ref[last : last + 1]
    ones = jnp.ones((8, length), BF16)
    for i in range(rows):
        for h in range(heads):
            score = st_ref[i, h] + bias_ref[h]
            top = jnp.max(score, axis=-1, keepdims=True)
            weights = jnp.exp2(score - top).astype(BF16)
            at = slice(h * PER_FOCUS_DIM, (h + 1) * PER_FOCUS_DIM)
            mixed = nt(v_ref[i, at, :], weights)
            total = nt(ones, weights)[0:1]
            out_ref[i, at, :] = (g_ref[i, at, :] * mixed / total).astype(BF16)


def transition_kernel(parts, own_only, *refs):
    heads_refs = refs[:parts]
    x_ref, wo_ref = refs[parts : parts + 2]
    count = 1 if own_only else parts
    entry_refs = refs[parts + 2 : parts + 2 + count]
    exit_refs = refs[parts + 2 + count : parts + 2 + 2 * count]
    out_ref, turn_ref = refs[-2:]
    seqs = x_ref.shape[0]
    features = heads_refs[0].shape[2]
    width = out_ref.shape[2]
    here = lax.axis_index("head")

    def owned(value):
        if parts == 2:
            return jnp.where(here == 0, value[:, :width], value[:, width:])
        turn_ref[...] = value.T
        return turn_ref[pl.ds(pl.multiple_of(here * width, width), width), :].T

    if own_only:
        begin = pl.multiple_of(here * width, width)
        weights = [(entry_refs[0][...], exit_refs[0][:, pl.ds(begin, width)])]
        for ref in refs[-4:-2]:
            units = ref.shape[0]
            weights.append((ref[:, :units], ref[:, units:]))
    else:
        weights = [(entry[...], leave[...]) for entry, leave in zip(entry_refs, exit_refs)]
    length = x_ref.shape[1]
    for begin_row in range(0, length, 128):
        at = slice(begin_row, begin_row + 128)
        blended = jnp.concatenate([x_ref[s, at, :] for s in range(seqs)], axis=0).astype(F32)
        for j in range(parts):
            which = jnp.where(j == 0, here, 1 - here) if parts == 2 else j
            begin = pl.multiple_of(which * features, features)
            mixed = jnp.concatenate([heads_refs[j][s, at, :] for s in range(seqs)], axis=0)
            blended = blended + nn(mixed, wo_ref[pl.ds(begin, features), :])
        standardized = normed(blended).astype(BF16)
        out = owned(blended)
        for enter, leave in weights:
            value = jnp.maximum(nn(standardized, enter), 0.0).astype(BF16)
            out = out + nn(value, leave)
        for s in range(seqs):
            out_ref[s, at, :] = out[s * 128 : (s + 1) * 128].astype(BF16)


def outer_kernel(cores, seqs, heads, *refs):
    found, (w_ref, share_ref, own_ref, out_ref, a_ref, b_ref) = sources(refs[:-6]), refs[-6:]
    doubling = len(refs) > 8
    rows, width, length = out_ref.shape
    depth = w_ref.shape[0]
    lanes = depth * cores * seqs
    groups = 128 // width
    steps = depth // groups
    total = len(found) * seqs
    core = lax.axis_index("branch")
    first = heads * rows
    last = first + seqs * depth
    lane_group = places((rows, lanes), 1) // depth
    slot = lax.axis_index("rows") % 4
    for at_source, (read, _, _) in enumerate(found):
        block = read(first, last).astype(F32)
        left = read(last, last + rows)[:, :lanes].astype(F32)
        if doubling:
            every = read(last, last + 4 * rows)[:, :lanes].astype(F32)
            for k in range(1, 4):
                left = jnp.where(slot == k, every[k * rows : (k + 1) * rows], left)
        for s in range(seqs):
            row = at_source * seqs + s
            for g in range(groups):
                begin = s * depth + g * steps
                for t in range(length // 128):
                    piece = block[begin : begin + steps, t * 128 : (t + 1) * 128]
                    b_ref[g, t, pl.ds(row, steps, stride=total), :] = piece
            kept = jnp.where(lane_group == core * seqs + s, left, 0.0)
            a_ref[pl.ds(row, rows, stride=total), :] = kept
    a = a_ref[...].astype(BF16)
    share = share_ref[...]
    gathered = [[] for _ in range(rows)]
    for step in range(steps):
        tile = jnp.concatenate([w_ref[:, step * 128 : (step + 1) * 128]] * (cores * seqs), axis=0)
        g = nn(a, tile).astype(BF16)
        for i in range(rows):
            gathered[i].append(g[i * total : (i + 1) * total])
    b = [[b_ref[g, t].T.astype(BF16) for t in range(length // 128)] for g in range(groups)]
    for i in range(rows):
        g = jnp.concatenate(gathered[i], axis=0)
        for t in range(length // 128):
            acc = None
            for k in range(groups):
                part = nn(b[k][t], g).T[k * width : (k + 1) * width]
                acc = part if acc is None else acc + part
            at = slice(t * 128, (t + 1) * 128)
            out_ref[i, :, at] = acc * share[i : i + 1, at] + own_ref[i, :, at].astype(F32)


def close_kernel(parts, *refs):
    heads_refs = refs[:parts]
    opm_ref, w_ref, fresh_ref, out_ref, copy_ref, stage_ref, sem = refs[parts:]
    copies = [
        pltpu.make_async_copy(fresh_ref, copy_ref, sem.at[0]),
        pltpu.make_async_copy(stage_ref, out_ref, sem.at[1]),
    ]
    copies[0].start()
    rows = opm_ref.shape[0]
    features = heads_refs[0].shape[1]
    own = lax.axis_index("head") == 0
    weight = w_ref[...]
    if parts == 2:
        first, second = weight[:, :features].astype(F32), weight[:, features:].astype(F32)
        turned = jnp.concatenate([second, first], axis=1)
        weight = jnp.where(own, weight.astype(F32), turned).astype(BF16)
    for i in range(rows):
        every = jnp.concatenate([ref[i] for ref in heads_refs], axis=0)
        stage_ref[i] = (opm_ref[i] + nn(weight, every)).astype(BF16)
    copies[1].start()
    for copy in copies:
        copy.wait()


def call(kernel, ins, outs, scratch=(), left=(), written=(), grant=0, flops=0):
    size = sum(a.size * a.dtype.itemsize for a in ins) + sum(
        math.prod(s) * jnp.dtype(d).itemsize for s, d in outs
    )
    held = sum(a.inner_aval.size * 4 for a in scratch )
    limit = grant or min(max((size + held) * 2, 8 << 20), 60 << 20)
    run = pl.pallas_call(
        kernel,
        compiler_params=pltpu.CompilerParams(vmem_limit_bytes=limit),
        out_shape=tuple(jax.ShapeDtypeStruct(s, d) for s, d in outs),
        in_specs=[HBM if i in left else VMEM for i in range(len(ins))],
        out_specs=tuple(HBM if i in written else VMEM for i in range(len(outs))),
        scratch_shapes=list(scratch),
        cost_estimate=pl.CostEstimate(flops=flops, bytes_accessed=size, transcendentals=0),
    )
    ins = [pltpu.with_memory_space_constraint(a, pltpu.HBM) if i in left else a for i, a in enumerate(ins)]
    return run(*ins)


def held_copies(arrays):
    return [*(pltpu.VMEM(a.shape, a.dtype) for a in arrays), pltpu.SemaphoreType.DMA((len(arrays),))]


def from_heads(value):
    if lax.axis_size("head") == 2:
        return [value, lax.ppermute(value, "head", [(0, 1), (1, 0)])]
    every = lax.all_gather(value, "head", axis=0)
    return [every[j] for j in range(every.shape[0])]


def local(
    lineup_state,
    pairwise,
    aligned_residue_bounds,
    residue_valid_mask,
    coupling_offset_weight_map,
    triangle_bias_matrix,
    alignment_projection_matrix,
    lineup_readout_weight,
    feedfwd_entry_weight,
    feedfwd_exit_weight,
    pair_projection_matrix,
    pair_output_matrix,
    left_right_maps,
    outer_product_output_matrix,
):
    seqs, length, channels = lineup_state.shape
    rows, _, pair_channels = pairwise.shape
    heads = coupling_offset_weight_map.shape[1]
    pair_heads = triangle_bias_matrix.shape[1]
    every_head = heads + pair_heads
    depth = left_right_maps.shape[2]
    chips = lax.axis_size("rows")
    cores = lax.axis_size("branch")
    parts = lax.axis_size("head")
    width = outer_product_output_matrix.shape[1]
    features = heads * PER_FOCUS_DIM
    pair_features = pair_heads * PER_FOCUS_DIM
    total = chips * cores * seqs
    bounds = aligned_residue_bounds.T

    first = (
        lineup_state,
        pairwise,
        coupling_offset_weight_map.T,
        triangle_bias_matrix.T,
        jnp.swapaxes(left_right_maps, 1, 2),
        bounds,
    )
    bias_rows = every_head * rows
    right_rows = seqs * depth
    hidden = feedfwd_entry_weight.shape[1]
    swap = [(0, 1), (1, 0)]
    packing = parts == 2 and cores == 2 and hidden == cores * channels
    pack_shape = (channels, hidden // cores + channels // parts)
    if chips == 8 and cores == 2:
        shape = (bias_rows + right_rows + chips // 2 * rows, length)
        outs = [(shape, BF16), (shape, BF16)]
        scratch = held_copies(first)
        if packing:
            first = (*first, feedfwd_entry_weight, feedfwd_exit_weight)
            outs.append((pack_shape, BF16))
            scratch.append(pltpu.SemaphoreType.DMA((2,)))
        near, far, *packed = call(
            functools.partial(pre_kernel, cores, True),
            first,
            outs,
            scratch=scratch,
            left=range(len(first)),
        )
        far = lax.ppermute(far, "rows", [(i, i ^ 4) for i in range(8)])
        both = jnp.concatenate([near, far], axis=0)
        mine = [both]
        for e in range(1, 4):
            mine.append(lax.ppermute(both, "rows", [(i, i ^ e) for i in range(8)]))
        other = []
        for e in range(4):
            other.append(lax.ppermute(mine[e], "branch", swap))
    else:
        (payload,) = call(
            functools.partial(pre_kernel, cores, False),
            first,
            (((chips, bias_rows + right_rows + rows, length), BF16),),
            scratch=[
                *held_copies(first)[:-1],
                pltpu.VMEM((chips, bias_rows, length), BF16),
                pltpu.VMEM((chips, right_rows + rows, length), BF16),
                held_copies(first)[-1],
                pltpu.SemaphoreType.DMA((2,)),
            ],
            left=range(len(first)),
            written=(0,),
            grant=60 << 20,
        )
        mine = [lax.all_to_all(payload, "rows", 0, 0, tiled=True)]
        other = [lax.ppermute(mine[0], "branch", swap)]

    if packing:
        if chips != 8:
            packed = call(
                pack_kernel,
                (feedfwd_entry_weight, feedfwd_exit_weight),
                ((pack_shape, BF16),),
                scratch=[pltpu.SemaphoreType.DMA((2,))],
                left=(0, 1),
            )
        others = [lax.ppermute(packed[0], "head", [(0, 1), (1, 0)])]
        others.append(lax.ppermute(others[0], "branch", [(0, 1), (1, 0)]))
        entries, exits = [feedfwd_entry_weight], [feedfwd_exit_weight]
    else:
        entries = lax.all_gather(feedfwd_entry_weight, "head", axis=0)
        exits = lax.all_to_all(feedfwd_exit_weight, "head", 1, 0, tiled=True)
        exits = exits.reshape(parts, -1, exits.shape[1])
        entries, exits, others = list(entries), list(exits), []

    groups = 128 // width
    second = (
        lineup_state,
        alignment_projection_matrix,
        bounds,
        residue_valid_mask.reshape(1, -1),
    )
    scores, values, gate, masks, shares = call(
        functools.partial(msa_kernel, cores, heads, rows),
        second,
        (
            ((seqs, heads, length, length), F32),
            ((seqs, length, features), BF16),
            ((seqs, length, features), F32),
            ((seqs + 1, length), F32),
            ((rows, length), F32),
        ),
        scratch=held_copies(second),
        left=range(len(second)),
        flops=1 << 28,
    )
    tri_scores, tri_values, tri_gate, own_pair, outer_w = call(
        functools.partial(pair_kernel, pair_heads),
        (
            pairwise,
            jnp.swapaxes(pair_projection_matrix, 1, 2),
            outer_product_output_matrix.T,
        ),
        (
            ((rows, pair_heads, length, length), F32),
            ((rows, pair_features, length), BF16),
            ((rows, pair_features, length), F32),
            ((rows, width, length), BF16),
            ((depth, depth * width), BF16),
        ),
        scratch=[
            pltpu.VMEM((pair_channels, length), F32),
            pltpu.VMEM((depth * depth, 128), F32),
        ],
        flops=1 << 28,
    )

    (mixed,) = call(
        functools.partial(align_kernel, cores, rows),
        (*mine, *other, scores, values, gate, masks),
        (((seqs, length, features), BF16),),
        scratch=[pltpu.VMEM((heads, length, length), F32)],
        flops=1 << 28,
    )
    mixed = from_heads(mixed)
    (pair_mixed,) = call(
        functools.partial(tri_kernel, cores, heads),
        (*mine, *other, tri_scores, tri_values, tri_gate, masks),
        (((rows, pair_features, length), BF16),),
        scratch=[pltpu.VMEM((pair_heads, length, length), F32)],
        flops=1 << 28,
    )
    pair_mixed = from_heads(pair_mixed)

    own_width = channels // parts
    (fresh,) = call(
        functools.partial(transition_kernel, parts, bool(others)),
        (*mixed, lineup_state, lineup_readout_weight, *entries, *exits, *others),
        (((seqs, length, own_width), BF16),),
        scratch=[pltpu.VMEM((channels, seqs * 128), F32)],
        flops=1 << 28,
    )

    (opm,) = call(
        functools.partial(outer_kernel, cores, seqs, every_head),
        (*mine, *other, outer_w, shares, own_pair),
        (((rows, width, length), F32),),
        scratch=[
            pltpu.VMEM((rows * total, depth * cores * seqs), F32),
            pltpu.VMEM((groups, length // 128, depth // groups * total, 128), F32),
        ],
        flops=1 << 28,
    )
    pair_out, refreshed = call(
        functools.partial(close_kernel, parts),
        (*pair_mixed, opm, pair_output_matrix.T, fresh),
        (((rows, width, length), BF16), (fresh.shape, BF16)),
        scratch=[pltpu.VMEM((rows, width, length), BF16), pltpu.SemaphoreType.DMA((2,))],
        written=(0, 1),
        flops=1 << 26,
    )
    return (refreshed, jnp.swapaxes(pair_out, 1, 2))


def solution(mesh):
    in_specs = (
        P(("parts", "rows", "branch"), None, None),
        P(("parts", "rows", "branch"), None, None),
        P("parts", None),
        P("parts"),
        P(None, "head"),
        P(None, "head"),
        P(None, None, "head"),
        P(),
        P(None, "head"),
        P("head", None),
        P(None, None, "head"),
        P(None, "head"),
        P(),
        P(None, "head"),
    )
    out_specs = (
        P(("parts", "rows", "branch"), None, "head"),
        P(("parts", "rows", "branch"), None, "head"),
    )


    return jax.shard_map(local, mesh=mesh, in_specs=in_specs, out_specs=out_specs, check_vma=False)
```

```python
import functools
import math

import jax
import jax.numpy as jnp
from jax import lax
from jax.experimental import pallas as pl
from jax.experimental.pallas import tpu as pltpu
from jax.sharding import PartitionSpec as P


PER_FOCUS_DIM = 32
F32 = jnp.float32
BF16 = jnp.bfloat16
LOG2E = math.log2(math.e)
SCALE = LOG2E / math.sqrt(PER_FOCUS_DIM)
FAR = -1.0e30

VMEM = pl.BlockSpec(memory_space=pltpu.VMEM)
HBM = pl.BlockSpec(memory_space=pltpu.HBM)


def nt(a, b):
    return lax.dot_general(a, b, (((1,), (1,)), ((), ())), preferred_element_type=F32)


def nn(a, b):
    return lax.dot_general(a, b, (((1,), (0,)), ((), ())), preferred_element_type=F32)


def normed(values):
    values = values.astype(F32)
    center = values - jnp.mean(values, -1, keepdims=True)
    spread = jnp.mean(center * center, -1, keepdims=True)
    return center * lax.rsqrt(spread + 1e-05)


def places(shape, axis):
    return lax.broadcasted_iota(jnp.int32, shape, axis)


def place_of(cores):
    return lax.axis_index("rows") * cores + lax.axis_index("branch")


def span_of(bounds_ref, which):
    bounds = bounds_ref[...].astype(F32)
    kept = jnp.where(places(bounds.shape, 1) == which, bounds, 0.0)
    span = jnp.sum(kept, axis=1, keepdims=True)
    return span[0:1], span[1:2]


def within(at, begin, end):
    at = at.astype(F32)
    return (at >= begin) & (at < end)


def fetch(pairs, sem):
    copies = [pltpu.make_async_copy(a, b, sem.at[j]) for j, (a, b) in enumerate(pairs)]
    for copy in copies:
        copy.start()
    return copies


def pack_copies(entry_ref, exit_ref, held_ref):
    units = held_ref.shape[0]
    width = held_ref.shape[1] - units
    first = pl.multiple_of(lax.axis_index("branch") * units, units)
    begin = pl.multiple_of((1 - lax.axis_index("head")) * width, width)
    return [
        (entry_ref.at[:, pl.ds(first, units)], held_ref.at[:, pl.ds(0, units)]),
        (exit_ref.at[pl.ds(first, units), pl.ds(begin, width)], held_ref.at[:, pl.ds(units, width)]),
    ]


def pack_kernel(entry_ref, exit_ref, out_ref, sem):
    for copy in fetch(pack_copies(entry_ref, exit_ref, out_ref), sem):
        copy.wait()


def pre_kernel(cores, doubling, *refs):
    packs = []
    if len(refs) > 15 and doubling:
        entry_ref, exit_ref, packed_ref, pack_sem = refs[6], refs[7], refs[10], refs[-1]
        refs = refs[:6] + refs[8:10] + refs[11:-1]
        packs = pack_copies(entry_ref, exit_ref, packed_ref)
    if doubling:
        (near_ref, far_ref), held, in_sem = refs[6:8], refs[8:14], refs[14]
        chips = 8
    else:
        pay_ref, held, (bias_ref, factor_ref, in_sem, out_sem) = refs[6], refs[7:13], refs[13:]
        chips = pay_ref.shape[0]
    copies = fetch(list(zip(refs[:6], held)), in_sem)
    if packs:
        packs = fetch(packs, pack_sem)
    x_ref, p_ref, mb_ref, tb_ref, lr_ref, bounds_ref = held
    seqs, length, _ = x_ref.shape
    rows = p_ref.shape[0]
    depth = lr_ref.shape[1]
    first_seq = place_of(cores) * seqs
    for j in (0, 4, 5):
        copies[j].wait()
    pieces = []
    left = None
    zero = jnp.zeros(lr_ref.shape[1:], BF16)
    for s in range(seqs):
        xn = normed(x_ref[s]).astype(BF16)
        begin, end = span_of(bounds_ref, first_seq + s)
        seen = within(places((1, length), 1), begin, end)
        pieces.append(nt(lr_ref[1], xn) * seen.astype(F32))
        weight = jnp.concatenate(
            [lr_ref[0] if other == s else zero for _ in range(cores) for other in range(seqs)],
            axis=0,
        )
        term = nt(xn, weight) * within(places((length, 1), 0), begin, end).astype(F32)
        left = term if left is None else left + term
    right = jnp.concatenate(pieces, axis=0).astype(BF16)
    lanes = left.shape[1]
    group = places((rows, lanes), 1) // (seqs * depth)
    first, count = (mb_ref.shape[0] + tb_ref.shape[0]) * rows, right.shape[0]
    lefts = []
    for d in range(chips):
        mine = left[d * cores * rows : d * cores * rows + rows]
        for c in range(1, cores):
            begin = (d * cores + c) * rows
            mine = jnp.where(group == c, left[begin : begin + rows], mine)
        if lanes < length:
            mine = jnp.concatenate([mine, jnp.zeros((rows, length - lanes), F32)], axis=1)
        lefts.append(mine)
    if doubling:
        low = lax.axis_index("rows") < chips // 2
        for k, ref in enumerate((near_ref, far_ref)):
            ref[first : first + count, :] = right
            half = chips // 2
            both = [(lefts[j], lefts[half + j])[:: 1 - 2 * k] for j in range(half)]
            chosen = jnp.concatenate([jnp.where(low, x, y) for x, y in both], axis=0)
            ref[first + count : first + count + half * rows, :] = chosen.astype(BF16)
    else:
        for d in range(chips):
            factor_ref[d, 0:count, :] = right
            factor_ref[d, count : count + rows, :] = lefts[d].astype(BF16)
        sends = [pltpu.make_async_copy(factor_ref, pay_ref.at[:, first:], out_sem.at[0])]
        sends[0].start()
    for j in (1, 2, 3):
        copies[j].wait()
    bias_w = jnp.concatenate([mb_ref[...].astype(F32), tb_ref[...].astype(F32)], axis=0)
    bias_w = bias_w.astype(BF16)
    heads = bias_w.shape[0]
    biases = [nt(bias_w, normed(p_ref[i]).astype(BF16)) for i in range(rows)]
    pieces = [jnp.concatenate([b[h : h + 1] for b in biases], axis=0) for h in range(heads)]
    bias = jnp.concatenate(pieces, axis=0).astype(BF16)
    if doubling:
        near_ref[0:first, :] = bias
        far_ref[0:first, :] = bias
        for copy in packs:
            copy.wait()
        return
    for d in range(chips):
        bias_ref[d] = bias
    sends.append(pltpu.make_async_copy(bias_ref, pay_ref.at[:, 0:first], out_sem.at[1]))
    sends[1].start()
    for copy in sends:
        copy.wait()


def msa_kernel(cores, heads, rows, x_ref, aw_ref, bounds_in, valid_in, *refs):
    sm_ref, v_ref, g_ref, mask_ref, share_ref, bounds_ref, valid_ref, sem = refs
    copies = fetch([(bounds_in, bounds_ref), (valid_in, valid_ref)], sem)
    seqs, length, _ = x_ref.shape
    for s in range(seqs):
        xn = normed(x_ref[s]).astype(BF16)
        q = nn(xn, aw_ref[0]).astype(BF16)
        k = nn(xn, aw_ref[1]).astype(BF16)
        v_ref[s] = nn(xn, aw_ref[2]).astype(BF16)
        g_ref[s] = jax.nn.sigmoid(nn(xn, aw_ref[3]))
        head = places(q.shape, 1) // PER_FOCUS_DIM
        for h in range(heads):
            sm_ref[s, h] = nt(jnp.where(head == h, q, jnp.zeros_like(q)), k) * SCALE
    for copy in copies:
        copy.wait()
    first_seq = place_of(cores) * seqs
    for s in range(seqs):
        begin, end = span_of(bounds_ref, first_seq + s)
        mask_ref[s : s + 1] = jnp.where(within(places((1, length), 1), begin, end), 0.0, FAR)
    mask_ref[seqs : seqs + 1] = jnp.where(valid_ref[...] > 0, 0.0, FAR)
    begin, end = bounds_ref[0:1].astype(F32), bounds_ref[1:2].astype(F32)
    whole = within(places((length, 1), 0), begin, end).astype(BF16)
    owned = within(places((rows, 1), 0) + place_of(cores) * rows, begin, end).astype(BF16)
    share_ref[...] = 1.0 / nt(owned, whole)


def pair_kernel(pair_heads, p_ref, pw_ref, ow_ref, st_ref, pv_ref, pg_ref, own_ref, lay_ref, turn_ref, rows_ref):
    rows = p_ref.shape[0]
    width = own_ref.shape[1]
    begin = pl.multiple_of(lax.axis_index("head") * width, width)
    for i in range(rows):
        pn = normed(p_ref[i]).astype(BF16)
        q = nt(pn, pw_ref[0]).astype(BF16)
        k = nt(pn, pw_ref[1]).astype(BF16)
        pv_ref[i] = nt(pw_ref[2], pn).astype(BF16)
        pg_ref[i] = jax.nn.sigmoid(nt(pw_ref[3], pn))
        head = places(q.shape, 1) // PER_FOCUS_DIM
        for h in range(pair_heads):
            st_ref[i, h] = nt(jnp.where(head == h, q, jnp.zeros_like(q)), k) * SCALE
        turn_ref[...] = p_ref[i].astype(F32).T
        own_ref[i] = turn_ref[pl.ds(begin, width), :].astype(BF16)
    groups = 128 // width
    steps = lay_ref.shape[1] // 128
    depth = steps * groups
    turned = ow_ref[...].astype(F32)
    rows_ref[...] = jnp.concatenate([turned] * groups, axis=0).T
    group = places((depth, 128), 1) // width
    for step in range(steps):
        tile = rows_ref[pl.ds(step, depth, stride=depth), :]
        for g in range(1, groups):
            part = rows_ref[pl.ds(g * steps + step, depth, stride=depth), :]
            tile = jnp.where(group == g, part, tile)
        lay_ref[:, step * 128 : (step + 1) * 128] = tile.astype(BF16)


def sources(refs):
    core = lax.axis_index("branch")
    half = len(refs) // 2
    pairs = list(zip(refs[:half], refs[half:]))
    found = []
    if half == 1:
        for d in range(refs[0].shape[0]):
            for ref, c in zip(pairs[0], (core, 1 - core)):
                found.append((lambda lo, hi, ref=ref, d=d: ref[d, lo:hi, :], d, c))
        return found
    chip = lax.axis_index("rows")
    for e, pair in enumerate(pairs):
        count = pair[0].shape[0] // 2
        for k in range(2):
            for ref, c in zip(pair, (core, 1 - core)):
                read = lambda lo, hi, ref=ref, at=k * count: ref[at + lo : at + hi, :]
                found.append((read, chip ^ (e + 4 * k), c))
    return found


def gather_bias(bias_ref, refs, first, heads, rows, cores):
    for read, d, c in sources(refs):
        begin = pl.multiple_of((d * cores + c) * rows, rows)
        block = read(first * rows, (first + heads) * rows).astype(F32) * LOG2E
        for h in range(heads):
            bias_ref[h, pl.ds(begin, rows), :] = block[h * rows : (h + 1) * rows]


def attend(scores, values, gate):
    width = values.shape[1]
    head = places(values.shape, 1) // PER_FOCUS_DIM
    mixed = total = None
    for h, score in enumerate(scores):
        top = jnp.max(score, axis=-1, keepdims=True)
        weights = jnp.exp2(score - top).astype(BF16)
        here = head == h
        value = jnp.where(here, values, jnp.zeros_like(values))
        ones = jnp.where(here, jnp.ones_like(values), jnp.zeros_like(values))
        if width % 128 == 0:
            both = nn(weights, jnp.concatenate([value, ones], axis=1))
            part, norm = both[:, :width], both[:, width:]
        else:
            part, norm = nn(weights, value), nn(weights, ones)
        mixed = part if mixed is None else mixed + part
        total = norm if total is None else total + norm
    return gate * mixed / total


def align_kernel(cores, rows, *refs):
    gathered, (sm_ref, v_ref, g_ref, mask_ref, out_ref, bias_ref) = refs[:-6], refs[-6:]
    seqs, heads, _, _ = sm_ref.shape
    gather_bias(bias_ref, gathered, 0, heads, rows, cores)
    for s in range(seqs):
        mask = mask_ref[s : s + 1]
        scores = [sm_ref[s, h] + (bias_ref[h] + mask) for h in range(heads)]
        out_ref[s] = attend(scores, v_ref[s], g_ref[s]).astype(BF16)


def tri_kernel(cores, first, *refs):
    gathered, (st_ref, v_ref, g_ref, mask_ref, out_ref, bias_ref) = refs[:-6], refs[-6:]
    rows, heads, length, _ = st_ref.shape
    last = mask_ref.shape[0] - 1
    gather_bias(bias_ref, gathered, first, heads, rows, cores)
    for h in range(heads):
        bias_ref[h] = bias_ref[h] + mask_ref[last : last + 1]
    ones = jnp.ones((8, length), BF16)
    for i in range(rows):
        for h in range(heads):
            score = st_ref[i, h] + bias_ref[h]
            top = jnp.max(score, axis=-1, keepdims=True)
            weights = jnp.exp2(score - top).astype(BF16)
            at = slice(h * PER_FOCUS_DIM, (h + 1) * PER_FOCUS_DIM)
            mixed = nt(v_ref[i, at, :], weights)
            total = nt(ones, weights)[0:1]
            out_ref[i, at, :] = (g_ref[i, at, :] * mixed / total).astype(BF16)


def transition_kernel(parts, own_only, *refs):
    heads_refs = refs[:parts]
    x_ref, wo_ref = refs[parts : parts + 2]
    count = 1 if own_only else parts
    entry_refs = refs[parts + 2 : parts + 2 + count]
    exit_refs = refs[parts + 2 + count : parts + 2 + 2 * count]
    out_ref, turn_ref = refs[-2:]
    seqs = x_ref.shape[0]
    features = heads_refs[0].shape[2]
    width = out_ref.shape[2]
    here = lax.axis_index("head")

    def owned(value):
        if parts == 2:
            return jnp.where(here == 0, value[:, :width], value[:, width:])
        turn_ref[...] = value.T
        return turn_ref[pl.ds(pl.multiple_of(here * width, width), width), :].T

    if own_only:
        begin = pl.multiple_of(here * width, width)
        weights = [(entry_refs[0][...], exit_refs[0][:, pl.ds(begin, width)])]
        for ref in refs[-4:-2]:
            units = ref.shape[0]
            weights.append((ref[:, :units], ref[:, units:]))
    else:
        weights = [(entry[...], leave[...]) for entry, leave in zip(entry_refs, exit_refs)]
    length = x_ref.shape[1]
    for begin_row in range(0, length, 128):
        at = slice(begin_row, begin_row + 128)
        blended = jnp.concatenate([x_ref[s, at, :] for s in range(seqs)], axis=0).astype(F32)
        for j in range(parts):
            which = jnp.where(j == 0, here, 1 - here) if parts == 2 else j
            begin = pl.multiple_of(which * features, features)
            mixed = jnp.concatenate([heads_refs[j][s, at, :] for s in range(seqs)], axis=0)
            blended = blended + nn(mixed, wo_ref[pl.ds(begin, features), :])
        standardized = normed(blended).astype(BF16)
        out = owned(blended)
        for enter, leave in weights:
            value = jnp.maximum(nn(standardized, enter), 0.0).astype(BF16)
            out = out + nn(value, leave)
        for s in range(seqs):
            out_ref[s, at, :] = out[s * 128 : (s + 1) * 128].astype(BF16)


def outer_kernel(cores, seqs, heads, *refs):
    found, (w_ref, share_ref, own_ref, out_ref, a_ref, b_ref) = sources(refs[:-6]), refs[-6:]
    doubling = len(refs) > 8
    rows, width, length = out_ref.shape
    depth = w_ref.shape[0]
    lanes = depth * cores * seqs
    groups = 128 // width
    steps = depth // groups
    total = len(found) * seqs
    core = lax.axis_index("branch")
    first = heads * rows
    last = first + seqs * depth
    lane_group = places((rows, lanes), 1) // depth
    slot = lax.axis_index("rows") % 4
    for at_source, (read, _, _) in enumerate(found):
        block = read(first, last).astype(F32)
        left = read(last, last + rows)[:, :lanes].astype(F32)
        if doubling:
            every = read(last, last + 4 * rows)[:, :lanes].astype(F32)
            for k in range(1, 4):
                left = jnp.where(slot == k, every[k * rows : (k + 1) * rows], left)
        for s in range(seqs):
            row = at_source * seqs + s
            for g in range(groups):
                begin = s * depth + g * steps
                for t in range(length // 128):
                    piece = block[begin : begin + steps, t * 128 : (t + 1) * 128]
                    b_ref[g, t, pl.ds(row, steps, stride=total), :] = piece
            kept = jnp.where(lane_group == core * seqs + s, left, 0.0)
            a_ref[pl.ds(row, rows, stride=total), :] = kept
    a = a_ref[...].astype(BF16)
    share = share_ref[...]
    gathered = [[] for _ in range(rows)]
    for step in range(steps):
        tile = jnp.concatenate([w_ref[:, step * 128 : (step + 1) * 128]] * (cores * seqs), axis=0)
        g = nn(a, tile).astype(BF16)
        for i in range(rows):
            gathered[i].append(g[i * total : (i + 1) * total])
    b = [[b_ref[g, t].T.astype(BF16) for t in range(length // 128)] for g in range(groups)]
    for i in range(rows):
        g = jnp.concatenate(gathered[i], axis=0)
        for t in range(length // 128):
            acc = None
            for k in range(groups):
                part = nn(b[k][t], g).T[k * width : (k + 1) * width]
                acc = part if acc is None else acc + part
            at = slice(t * 128, (t + 1) * 128)
            out_ref[i, :, at] = acc * share[i : i + 1, at] + own_ref[i, :, at].astype(F32)


def close_kernel(parts, *refs):
    heads_refs = refs[:parts]
    opm_ref, w_ref, fresh_ref, out_ref, copy_ref, stage_ref, sem = refs[parts:]
    copies = [
        pltpu.make_async_copy(fresh_ref, copy_ref, sem.at[0]),
        pltpu.make_async_copy(stage_ref, out_ref, sem.at[1]),
    ]
    copies[0].start()
    rows = opm_ref.shape[0]
    features = heads_refs[0].shape[1]
    own = lax.axis_index("head") == 0
    weight = w_ref[...]
    if parts == 2:
        first, second = weight[:, :features].astype(F32), weight[:, features:].astype(F32)
        turned = jnp.concatenate([second, first], axis=1)
        weight = jnp.where(own, weight.astype(F32), turned).astype(BF16)
    for i in range(rows):
        every = jnp.concatenate([ref[i] for ref in heads_refs], axis=0)
        stage_ref[i] = (opm_ref[i] + nn(weight, every)).astype(BF16)
    copies[1].start()
    for copy in copies:
        copy.wait()


def call(kernel, ins, outs, scratch=(), left=(), written=(), grant=0, flops=0):
    size = sum(a.size * a.dtype.itemsize for a in ins) + sum(
        math.prod(s) * jnp.dtype(d).itemsize for s, d in outs
    )
    held = sum(a.inner_aval.size * 4 for a in scratch )
    limit = grant or min(max((size + held) * 2, 8 << 20), 60 << 20)
    run = pl.pallas_call(
        kernel,
        compiler_params=pltpu.CompilerParams(vmem_limit_bytes=limit),
        out_shape=tuple(jax.ShapeDtypeStruct(s, d) for s, d in outs),
        in_specs=[HBM if i in left else VMEM for i in range(len(ins))],
        out_specs=tuple(HBM if i in written else VMEM for i in range(len(outs))),
        scratch_shapes=list(scratch),
        cost_estimate=pl.CostEstimate(flops=flops, bytes_accessed=size, transcendentals=0),
    )
    ins = [pltpu.with_memory_space_constraint(a, pltpu.HBM) if i in left else a for i, a in enumerate(ins)]
    return run(*ins)


def held_copies(arrays):
    return [*(pltpu.VMEM(a.shape, a.dtype) for a in arrays), pltpu.SemaphoreType.DMA((len(arrays),))]


def from_heads(value):
    if lax.axis_size("head") == 2:
        return [value, lax.ppermute(value, "head", [(0, 1), (1, 0)])]
    every = lax.all_gather(value, "head", axis=0)
    return [every[j] for j in range(every.shape[0])]


def local(
    lineup_state,
    pairwise,
    aligned_residue_bounds,
    residue_valid_mask,
    coupling_offset_weight_map,
    triangle_bias_matrix,
    alignment_projection_matrix,
    lineup_readout_weight,
    feedfwd_entry_weight,
    feedfwd_exit_weight,
    pair_projection_matrix,
    pair_output_matrix,
    left_right_maps,
    outer_product_output_matrix,
):
    seqs, length, channels = lineup_state.shape
    rows, _, pair_channels = pairwise.shape
    heads = coupling_offset_weight_map.shape[1]
    pair_heads = triangle_bias_matrix.shape[1]
    every_head = heads + pair_heads
    depth = left_right_maps.shape[2]
    chips = lax.axis_size("rows")
    cores = lax.axis_size("branch")
    parts = lax.axis_size("head")
    width = outer_product_output_matrix.shape[1]
    features = heads * PER_FOCUS_DIM
    pair_features = pair_heads * PER_FOCUS_DIM
    total = chips * cores * seqs
    bounds = aligned_residue_bounds.T

    first = (
        lineup_state,
        pairwise,
        coupling_offset_weight_map.T,
        triangle_bias_matrix.T,
        jnp.swapaxes(left_right_maps, 1, 2),
        bounds,
    )
    bias_rows = every_head * rows
    right_rows = seqs * depth
    hidden = feedfwd_entry_weight.shape[1]
    swap = [(0, 1), (1, 0)]
    packing = parts == 2 and cores == 2 and hidden == cores * channels
    pack_shape = (channels, hidden // cores + channels // parts)
    if chips == 8 and cores == 2:
        shape = (bias_rows + right_rows + chips // 2 * rows, length)
        outs = [(shape, BF16), (shape, BF16)]
        scratch = held_copies(first)
        if packing:
            first = (*first, feedfwd_entry_weight, feedfwd_exit_weight)
            outs.append((pack_shape, BF16))
            scratch.append(pltpu.SemaphoreType.DMA((2,)))
        near, far, *packed = call(
            functools.partial(pre_kernel, cores, True),
            first,
            outs,
            scratch=scratch,
            left=range(len(first)),
        )
        far = lax.ppermute(far, "rows", [(i, i ^ 4) for i in range(8)])
        both = jnp.concatenate([near, far], axis=0)
        mine = [both]
        for e in range(1, 4):
            mine.append(lax.ppermute(both, "rows", [(i, i ^ e) for i in range(8)]))
        other = []
        for e in range(4):
            other.append(lax.ppermute(mine[e], "branch", swap))
    else:
        (payload,) = call(
            functools.partial(pre_kernel, cores, False),
            first,
            (((chips, bias_rows + right_rows + rows, length), BF16),),
            scratch=[
                *held_copies(first)[:-1],
                pltpu.VMEM((chips, bias_rows, length), BF16),
                pltpu.VMEM((chips, right_rows + rows, length), BF16),
                held_copies(first)[-1],
                pltpu.SemaphoreType.DMA((2,)),
            ],
            left=range(len(first)),
            written=(0,),
            grant=60 << 20,
        )
        mine = [lax.all_to_all(payload, "rows", 0, 0, tiled=True)]
        other = [lax.ppermute(mine[0], "branch", swap)]

    if packing:
        if chips != 8:
            packed = call(
                pack_kernel,
                (feedfwd_entry_weight, feedfwd_exit_weight),
                ((pack_shape, BF16),),
                scratch=[pltpu.SemaphoreType.DMA((2,))],
                left=(0, 1),
            )
        others = [lax.ppermute(packed[0], "head", [(0, 1), (1, 0)])]
        others.append(lax.ppermute(others[0], "branch", [(0, 1), (1, 0)]))
        entries, exits = [feedfwd_entry_weight], [feedfwd_exit_weight]
    else:
        entries = lax.all_gather(feedfwd_entry_weight, "head", axis=0)
        exits = lax.all_to_all(feedfwd_exit_weight, "head", 1, 0, tiled=True)
        exits = exits.reshape(parts, -1, exits.shape[1])
        entries, exits, others = list(entries), list(exits), []

    groups = 128 // width
    second = (
        lineup_state,
        alignment_projection_matrix,
        bounds,
        residue_valid_mask.reshape(1, -1),
    )
    scores, values, gate, masks, shares = call(
        functools.partial(msa_kernel, cores, heads, rows),
        second,
        (
            ((seqs, heads, length, length), F32),
            ((seqs, length, features), BF16),
            ((seqs, length, features), F32),
            ((seqs + 1, length), F32),
            ((rows, length), F32),
        ),
        scratch=held_copies(second[2:]),
        left=(2, 3),
        flops=1 << 28,
    )
    tri_scores, tri_values, tri_gate, own_pair, outer_w = call(
        functools.partial(pair_kernel, pair_heads),
        (
            pairwise,
            jnp.swapaxes(pair_projection_matrix, 1, 2),
            outer_product_output_matrix.T,
        ),
        (
            ((rows, pair_heads, length, length), F32),
            ((rows, pair_features, length), BF16),
            ((rows, pair_features, length), F32),
            ((rows, width, length), BF16),
            ((depth, depth * width), BF16),
        ),
        scratch=[
            pltpu.VMEM((pair_channels, length), F32),
            pltpu.VMEM((depth * depth, 128), F32),
        ],
        flops=1 << 28,
    )

    (mixed,) = call(
        functools.partial(align_kernel, cores, rows),
        (*mine, *other, scores, values, gate, masks),
        (((seqs, length, features), BF16),),
        scratch=[pltpu.VMEM((heads, length, length), F32)],
        flops=1 << 28,
    )
    mixed = from_heads(mixed)
    (pair_mixed,) = call(
        functools.partial(tri_kernel, cores, heads),
        (*mine, *other, tri_scores, tri_values, tri_gate, masks),
        (((rows, pair_features, length), BF16),),
        scratch=[pltpu.VMEM((pair_heads, length, length), F32)],
        flops=1 << 28,
    )
    pair_mixed = from_heads(pair_mixed)

    own_width = channels // parts
    (fresh,) = call(
        functools.partial(transition_kernel, parts, bool(others)),
        (*mixed, lineup_state, lineup_readout_weight, *entries, *exits, *others),
        (((seqs, length, own_width), BF16),),
        scratch=[pltpu.VMEM((channels, seqs * 128), F32)],
        flops=1 << 28,
    )

    (opm,) = call(
        functools.partial(outer_kernel, cores, seqs, every_head),
        (*mine, *other, outer_w, shares, own_pair),
        (((rows, width, length), F32),),
        scratch=[
            pltpu.VMEM((rows * total, depth * cores * seqs), F32),
            pltpu.VMEM((groups, length // 128, depth // groups * total, 128), F32),
        ],
        flops=1 << 28,
    )
    pair_out, refreshed = call(
        functools.partial(close_kernel, parts),
        (*pair_mixed, opm, pair_output_matrix.T, fresh),
        (((rows, width, length), BF16), (fresh.shape, BF16)),
        scratch=[pltpu.VMEM((rows, width, length), BF16), pltpu.SemaphoreType.DMA((2,))],
        written=(0, 1),
        flops=1 << 26,
    )
    return (refreshed, jnp.swapaxes(pair_out, 1, 2))


def solution(mesh):
    in_specs = (
        P(("parts", "rows", "branch"), None, None),
        P(("parts", "rows", "branch"), None, None),
        P("parts", None),
        P("parts"),
        P(None, "head"),
        P(None, "head"),
        P(None, None, "head"),
        P(),
        P(None, "head"),
        P("head", None),
        P(None, None, "head"),
        P(None, "head"),
        P(),
        P(None, "head"),
    )
    out_specs = (
        P(("parts", "rows", "branch"), None, "head"),
        P(("parts", "rows", "branch"), None, "head"),
    )


    return jax.shard_map(local, mesh=mesh, in_specs=in_specs, out_specs=out_specs, check_vma=False)
```
